32 devices in a mesh: groups: 1, tok: 8 (over z, y), exp: 2 (over x), sub: 2 (over core).
Axes of the slice: x: 2, y: 2, z: 4, core: 2. Of those that a mesh axis runs over, the one named last changes fastest.
Arguments:
- query: bfloat16 [2, 2, 4, 4096], P(('groups', 'sub'), 'exp'), may hold values from -9 to 9, as said below
- key_cache_table: bfloat16 [2, 2, 4, 1024, 512], P(('groups', 'sub'), 'exp', None, 'tok'), may hold values from -9 to 9, as said below
- value_cache_table: bfloat16 [2, 2, 4, 1024, 512], P(('groups', 'sub'), 'exp', None, 'tok'), may hold values from -6 to 6
- latest_key: bfloat16 [2, 2, 4, 512], P(('groups', 'sub'), 'exp'), may hold values from -6 to 6
- latest_value: bfloat16 [2, 2, 4, 512], P(('groups', 'sub'), 'exp'), may hold values from -6 to 6
- lengths: int32 [2, 2, 4], P(('groups', 'sub'), 'exp'), may hold values from 2 to 1024, as said below
- resid: bfloat16 [2, 2, 4, 2048], P(('groups', 'sub'), 'exp', None, 'tok'), may hold values from -250 to 250
- norm_gain: float32 [2048], replicated, may hold values from 0.5 to 1.5
- out_weight: bfloat16 [4096, 2048], P('tok'), may hold values from -0.09375 to 0.09375
- expert_ids: int32 [2, 2, 4, 8], P('groups'), may hold values from 0 to 15, all different within a row; in each aligned block of 16 rows (0 to 15, 16 to 31, ..., all dimensions but the last counted through in order) at most 16 rows name the same one
- gate_weights: float32 [2, 2, 4, 8], P('groups'), may hold values from 0.05 to 0.35
- w_gate: bfloat16 [16, 2048, 768], P(('tok', 'sub'), None, 'exp'), may hold values from -0.125 to 0.125
- w_up: bfloat16 [16, 2048, 768], P(('tok', 'sub'), None, 'exp'), may hold values from -0.125 to 0.125
- w_down: bfloat16 [16, 768, 2048], P(('tok', 'sub'), 'exp'), may hold values from -0.21875 to 0.21875
Outputs:
- attention_out: float32 [2, 2, 4, 2048], P(('groups', 'sub'), 'exp', None, 'tok')
- expert_out: float32 [2, 2, 4, 2048], P('groups', None, None, ('tok', 'exp', 'sub'))
The draws below stay inside these ranges and needn't reach their ends.
Inputs may be any that keep to these rules, and one draw needn't show every extreme that they name: `query`: most entries are of order one; some rows may align queries of the first key head's query heads with the keys at positions 0 and 1. `key_cache_table`: most entries are of order one. `lengths`: some row reaches 1024. `expert_ids`: each row names 8 different experts; over all 16 rows no expert is named by more than 16 rows, a bound that some block reaches.
All inputs are finite; a program needn't handle non-finite values.
Results may differ from the reference program's by a relative error of at most 0.013.
Values may be sent and summed in bfloat16 or wider, within the bound.
No kernel may reach another device: no remote copies, remote signals or barrier semaphores. Data moves between devices by JAX's collectives and lax.ppermute only.
A program may use at most 64 MiB of HBM per device.

```python
import math
import jax
import jax.numpy as jnp
import numpy as np
from jax import lax

D = 2048
QUERY_HEADS = 32
KEY_VALUE_HEADS = 4
HEAD_DIMENSION = 128
FFE = 768
TOPK = 8
SEQUENCE_COUNT = 4
CONTEXT_LOCAL = 128
SUBGROUP_INDEX = 2
EXPERT_INDEX = 2
ROWS_ALL = 16
EXPERTS = 16
CAP = 16
CONTEXT_TOTAL = 1024
N_TOK = 8


def draw_query(key, part):
    count_of_rows = SUBGROUP_INDEX * EXPERT_INDEX * SEQUENCE_COUNT
    sample_entry = jax.random.truncated_normal(jax.random.fold_in(key, 11), -6.0, 6.0, (count_of_rows, QUERY_HEADS, HEAD_DIMENSION), jnp.float32)
    return sample_entry.reshape(SUBGROUP_INDEX, EXPERT_INDEX, SEQUENCE_COUNT, QUERY_HEADS * HEAD_DIMENSION).astype(jnp.bfloat16)


def draw_key_cache_table(key, part):
    count_of_rows = SUBGROUP_INDEX * EXPERT_INDEX * SEQUENCE_COUNT
    sample_entry = jax.random.truncated_normal(jax.random.fold_in(key, 23), -6.0, 6.0, (count_of_rows, CONTEXT_TOTAL, KEY_VALUE_HEADS, HEAD_DIMENSION), jnp.float32)
    return sample_entry.reshape(SUBGROUP_INDEX, EXPERT_INDEX, SEQUENCE_COUNT, CONTEXT_TOTAL, KEY_VALUE_HEADS * HEAD_DIMENSION).astype(jnp.bfloat16)


def draw_lengths(key, part):
    sample_entry = jax.random.randint(jax.random.fold_in(key, 31), (SUBGROUP_INDEX, EXPERT_INDEX, SEQUENCE_COUNT), 2, CONTEXT_TOTAL + 1, dtype=jnp.int32)
    return sample_entry.at[0, 0, 0].set(CONTEXT_TOTAL)


def draw_resid(key, part):
    count_of_rows = SUBGROUP_INDEX * EXPERT_INDEX * SEQUENCE_COUNT
    first_key = jax.random.fold_in(key, 41)
    second_key = jax.random.fold_in(key, 43)
    third_key = jax.random.fold_in(key, 47)
    sample_entry = jax.random.truncated_normal(first_key, -6.0, 6.0, (count_of_rows, D), jnp.float32)
    column_scale = 3.0 ** (jnp.arange(D, dtype=jnp.float32) / D) * jnp.exp(jax.random.uniform(second_key, (D,), jnp.float32, -0.2, 0.2))
    row_scale = jnp.exp(jax.random.uniform(third_key, (count_of_rows, 1), jnp.float32, 0.0, math.log(10.0)))
    sample_entry = sample_entry * column_scale[None, :] * row_scale
    return sample_entry.reshape(SUBGROUP_INDEX, EXPERT_INDEX, SEQUENCE_COUNT, D).astype(jnp.bfloat16)


def block_levels(key, shape, cuts, smallest, high):
    gain, own = 1.0, jax.random.fold_in(key, 6)
    for dim, shards_of in cuts:
        steps = jnp.exp(jax.random.uniform(jax.random.fold_in(own, dim), (shards_of,), jnp.float32, smallest / len(cuts), high / len(cuts)))
        gain = gain * jnp.repeat(steps, shape[dim] // shards_of).reshape([-1 if axis == dim else 1 for axis in range(len(shape))])
    return gain


def shared_out(rng, own, number, rows, number_of, top, most, lean):
    sequence = jax.random.permutation(rng, number_of)
    heavy_load, common = load_shares(number_of, rows * top, most, lean, True), load_shares(number_of, rows * top, most, lean, False)
    places = jnp.arange(number_of)

    def named(sizes, turn):
        used = int((sizes > 0).sum())
        fixed = max(1, used // 4)
        passed = fixed + (places - fixed + turn * (used - fixed)) % max(1, number_of - fixed)
        return jnp.zeros((number_of,), jnp.int32).at[sequence[jnp.where(places < fixed, places, passed)]].set(jnp.asarray(sizes, jnp.int32))

    sizes = jnp.where(number % 4 == 0, named(heavy_load, number // 4), named(common, number - number // 4 - 1))
    mixed = jax.random.permutation(jax.random.fold_in(own, 3), number_of)
    giver, taker = mixed[0:number_of // 2 * 2:2], mixed[1:number_of // 2 * 2:2]
    slack = jnp.minimum(sizes[giver] - 1, most - sizes[taker]) // 2
    slack = jnp.where((giver == sequence[0]) | (taker == sequence[0]) | (sizes[taker] == 0), 0, jnp.maximum(slack, 0))
    passed = jax.random.randint(jax.random.fold_in(own, 4), (number_of // 2,), 0, 1 << 20) % (slack + 1)
    sizes = sizes.at[giver].add(-passed).at[taker].add(passed)
    labels = jnp.searchsorted(jnp.cumsum(sizes), jnp.arange(rows * top), side="right").astype(jnp.int32)
    listing = labels.reshape(top, rows).T
    listing = listing[jax.random.permutation(jax.random.fold_in(own, 1), rows)]
    turn = jax.random.randint(jax.random.fold_in(own, 2), (rows, 1), 0, top)
    return jnp.take_along_axis(listing, (jnp.arange(top)[None, :] + turn) % top, axis=1)


def load_shares(number_of, total, reach, lean, full):
    portions = [(1 << 20) // math.isqrt(rank ** lean) + 1 for rank in range(1, number_of + 1)]
    largest = reach if full else min(reach, max(-(-total // number_of), total * portions[0] // sum(portions)))
    least = 1 if total - largest >= number_of - 1 else 0
    given, spare = [largest] + [least] * (number_of - 1), total - largest - least * (number_of - 1)
    while spare > 0:
        free = [i for i in range(1, number_of) if given[i] < largest] or [i for i in range(1, number_of) if given[i] < reach]
        mass, remaining = sum([portions[i] for i in free]), spare
        for i in free:
            addition = min(reach - given[i], max(1, remaining * portions[i] // mass), spare)
            given[i] = given[i] + addition
            spare = spare - addition
    return np.array(given)


def centred(own_key, extent, scale, bound, split=(), kind=jnp.bfloat16):
    drawn = jax.random.normal(own_key, extent, jnp.float32) * scale
    if len(split) > 0:
        drawn = block_levels(own_key, extent, split, -0.22, 0.18) * drawn
    return jnp.clip(drawn, min=-bound, max=bound).astype(kind)


def setup_inputs(seed: int = 0, part: int = 0) -> dict:
    splits = jax.random.split(jax.random.key(seed), 15)
    own_keys = jax.random.split(jax.random.fold_in(splits[14], part), 15)
    query = draw_query(jax.random.fold_in(jax.random.fold_in(splits[14], part), 71), part)
    key_cache_table = draw_key_cache_table(jax.random.fold_in(jax.random.fold_in(splits[14], part), 71), part)
    value_cache_table = centred(own_keys[2], (SUBGROUP_INDEX, EXPERT_INDEX, SEQUENCE_COUNT, CONTEXT_TOTAL, KEY_VALUE_HEADS * HEAD_DIMENSION), 1.0, 6.0, ((0, 2), (1, 2), (3, 8)))
    latest_key = centred(own_keys[3], (SUBGROUP_INDEX, EXPERT_INDEX, SEQUENCE_COUNT, KEY_VALUE_HEADS * HEAD_DIMENSION), 1.0, 6.0, ((0, 2), (1, 2)))
    latest_value = centred(own_keys[4], (SUBGROUP_INDEX, EXPERT_INDEX, SEQUENCE_COUNT, KEY_VALUE_HEADS * HEAD_DIMENSION), 1.0, 6.0, ((0, 2), (1, 2)))
    lengths = draw_lengths(jax.random.fold_in(jax.random.fold_in(splits[14], part), 71), part)
    resid = draw_resid(jax.random.fold_in(jax.random.fold_in(splits[14], part), 71), part)
    norm_gain = jnp.clip(1.0 + 0.1 * jax.random.normal(splits[7], (D,), jnp.float32), 0.5, 1.5)
    out_weight = centred(splits[8], (QUERY_HEADS * HEAD_DIMENSION, D), (QUERY_HEADS * HEAD_DIMENSION) ** -0.5, 0.09375, ((0, 8),))
    expert_ids_keys = jax.random.split(jax.random.fold_in(own_keys[9], 1), SUBGROUP_INDEX * EXPERT_INDEX * SEQUENCE_COUNT // ROWS_ALL)
    expert_ids_turns = jax.random.permutation(jax.random.fold_in(own_keys[9], 3), SUBGROUP_INDEX * EXPERT_INDEX * SEQUENCE_COUNT // ROWS_ALL)
    expert_ids = jax.vmap(lambda own, number: shared_out(jax.random.fold_in(own_keys[9], 2), own, number, ROWS_ALL, EXPERTS, TOPK, CAP, 2))(expert_ids_keys, expert_ids_turns).reshape((SUBGROUP_INDEX, EXPERT_INDEX, SEQUENCE_COUNT, TOPK))
    gate_weights = jnp.clip(jax.random.uniform(own_keys[10], (SUBGROUP_INDEX, EXPERT_INDEX, SEQUENCE_COUNT, TOPK), jnp.float32, 0.05, 0.35), 0.05, 0.35)
    w_gate = centred(splits[11], (EXPERTS, D, FFE), D ** -0.5, 0.125, ((0, 16), (2, 2)))
    w_up = centred(splits[12], (EXPERTS, D, FFE), D ** -0.5, 0.125, ((0, 16), (2, 2)))
    w_down = centred(splits[13], (EXPERTS, FFE, D), FFE ** -0.5, 0.21875, ((0, 16), (1, 2)))
    return {"query": query, "key_cache_table": key_cache_table, "value_cache_table": value_cache_table, "latest_key": latest_key, "latest_value": latest_value, "lengths": lengths, "resid": resid, "norm_gain": norm_gain, "out_weight": out_weight, "expert_ids": expert_ids, "gate_weights": gate_weights, "w_gate": w_gate, "w_up": w_up, "w_down": w_down}


def attend_single_row(packed):
    query_per_row, keys_per_row, values_per_row, incoming_key, incoming_value, row_length = packed
    query_group_width = QUERY_HEADS // KEY_VALUE_HEADS
    score_scale = HEAD_DIMENSION ** (-0.5)
    query_rows = query_per_row.reshape(KEY_VALUE_HEADS, query_group_width, HEAD_DIMENSION).astype(jnp.float32)
    stored_keys = keys_per_row.reshape(N_TOK, CONTEXT_LOCAL, KEY_VALUE_HEADS, HEAD_DIMENSION).astype(jnp.float32)
    stored_values = values_per_row.reshape(N_TOK, CONTEXT_LOCAL, KEY_VALUE_HEADS, HEAD_DIMENSION).astype(jnp.float32)
    scores = jnp.einsum('hgd,bphd->bhgp', query_rows, stored_keys) * score_scale
    position = lax.broadcasted_iota(jnp.int32, (N_TOK, 1, 1, CONTEXT_LOCAL), 0) * CONTEXT_LOCAL + lax.broadcasted_iota(jnp.int32, (N_TOK, 1, 1, CONTEXT_LOCAL), 3)
    usable = position < row_length
    masked = jnp.where(usable, scores, -1e+30)
    block_max = lax.optimization_barrier(jnp.max(masked, axis=3))
    weights = jnp.where(usable, jnp.exp(masked - block_max[..., None]), 0.0).astype(jnp.bfloat16)
    weights = weights.astype(jnp.float32)
    totals = lax.optimization_barrier(jnp.sum(weights, axis=3))
    numerator = jnp.einsum('bhgp,bphd->bhgd', weights, stored_values)
    partial_value = (numerator / jnp.maximum(totals, 1.0)[..., None]).astype(jnp.bfloat16).astype(jnp.float32)
    device_key = incoming_key.reshape(KEY_VALUE_HEADS, HEAD_DIMENSION).astype(jnp.float32)
    device_value = incoming_value.reshape(KEY_VALUE_HEADS, 1, HEAD_DIMENSION).astype(jnp.float32)
    own_score = jnp.einsum('hgd,hd->hg', query_rows, device_key) * score_scale
    top_score = jnp.maximum(lax.optimization_barrier(jnp.max(block_max, axis=0)), own_score)
    factor = totals * jnp.exp(block_max - top_score[None])
    self_weight = jnp.exp(own_score - top_score)
    combined = jnp.einsum('bhg,bhgd->hgd', factor, partial_value) + self_weight[..., None] * device_value
    heads_out = combined / (lax.optimization_barrier(jnp.sum(factor, axis=0)) + self_weight)[..., None]
    return heads_out.reshape(QUERY_HEADS * HEAD_DIMENSION).astype(jnp.bfloat16)

def reference(query, key_cache_table, value_cache_table, latest_key, latest_value, lengths, resid, norm_gain, out_weight, expert_ids, gate_weights, w_gate, w_up, w_down):
    count_of_rows = ROWS_ALL
    every_head = lax.map(attend_single_row, (query.reshape(count_of_rows, QUERY_HEADS * HEAD_DIMENSION), key_cache_table.reshape(count_of_rows, CONTEXT_TOTAL, KEY_VALUE_HEADS * HEAD_DIMENSION), value_cache_table.reshape(count_of_rows, CONTEXT_TOTAL, KEY_VALUE_HEADS * HEAD_DIMENSION), latest_key.reshape(count_of_rows, KEY_VALUE_HEADS * HEAD_DIMENSION), latest_value.reshape(count_of_rows, KEY_VALUE_HEADS * HEAD_DIMENSION), lengths.reshape(count_of_rows)))
    attended = jnp.dot(every_head, out_weight, preferred_element_type=jnp.float32)
    hidden_state = resid.reshape(count_of_rows, D).astype(jnp.float32) + attended
    normed = (hidden_state * lax.rsqrt(lax.optimization_barrier(jnp.mean(hidden_state * hidden_state, axis=1, keepdims=True)) + 1e-06) * norm_gain.astype(jnp.float32)).astype(jnp.bfloat16)
    chosen_ids = expert_ids.reshape(count_of_rows, TOPK)
    chosen_gates = gate_weights.reshape(count_of_rows, TOPK).astype(jnp.float32)

    def expert_step(running, packed):
        expert_idx, gate_mat, up_mat, down_mat = packed
        gate_proj = jnp.dot(normed, gate_mat, preferred_element_type=jnp.float32)
        up_proj = jnp.dot(normed, up_mat, preferred_element_type=jnp.float32)
        active = (jax.nn.silu(gate_proj) * up_proj).astype(jnp.bfloat16)
        output = jnp.dot(active, down_mat, preferred_element_type=jnp.float32).astype(jnp.bfloat16)
        output = lax.optimization_barrier(output).astype(jnp.float32)
        weight_sum = lax.optimization_barrier(jnp.sum(jnp.where(chosen_ids == expert_idx, chosen_gates, 0.0), axis=1))
        return (running + weight_sum[:, None] * output, None)
    expert_mix, _ = lax.scan(expert_step, jnp.zeros((count_of_rows, D), jnp.float32), (jnp.arange(EXPERTS, dtype=jnp.int32), w_gate, w_up, w_down))
    row_shape = (SUBGROUP_INDEX, EXPERT_INDEX, SEQUENCE_COUNT, D)
    return (attended.reshape(row_shape), expert_mix.reshape(row_shape))
```

```python
import functools

import jax
import jax.numpy as jnp
from jax import lax
from jax.experimental import pallas as pl
from jax.experimental.pallas import tpu as pltpu
from jax.sharding import PartitionSpec as P

D = 2048
QUERY_HEADS = 32
KEY_VALUE_HEADS = 4
HEAD_DIMENSION = 128
TOPK = 8
GROUP = QUERY_HEADS // KEY_VALUE_HEADS
SCALE = HEAD_DIMENSION ** (-0.5)
LANES = 128
HALF = 64

F32 = jnp.float32
BF16 = jnp.bfloat16


def attend_kernel(len_ref, q_ref, resid_ref, k_hbm, v_hbm, msg_ref, kbuf, vbuf, qs, tail, sems):
    rows = q_ref.shape[0]
    extent = k_hbm.shape[1]
    own_heads = resid_ref.shape[1] // HALF
    block = GROUP * rows
    copies = []
    for which, (source, target) in enumerate(((k_hbm, kbuf), (v_hbm, vbuf))):
        for r in range(rows):
            copy = pltpu.make_async_copy(
                source.at[r], target.at[pl.ds(r * extent, extent)], sems.at[which, r]
            )
            copy.start()
            copies.append(copy)
    for h in range(QUERY_HEADS):
        qs[rows * h : rows * (h + 1), :] = q_ref[
            :, HEAD_DIMENSION * h : HEAD_DIMENSION * (h + 1)
        ].astype(F32)
    tail[...] = jnp.zeros_like(tail)
    for j in range(own_heads):
        tail[rows * j : rows * (j + 1), HALF:LANES] = resid_ref[
            :, HALF * j : HALF * (j + 1)
        ].astype(F32)
    row_id = lax.rem(lax.broadcasted_iota(jnp.int32, (block, 1), 0), rows)
    limit = jnp.zeros((block, 1), jnp.int32)
    for r in range(rows):
        limit = jnp.where(row_id == r, len_ref[0, 0, r], limit)
    first = lax.axis_index("tok") * extent
    usable = first + lax.broadcasted_iota(jnp.int32, (block, extent), 1) < limit
    lane = lax.broadcasted_iota(jnp.int32, (block, LANES), 1)
    per = own_heads * rows
    spread = jnp.concatenate([tail[...]] * (block // per), axis=0)
    for copy in copies[:rows]:
        copy.wait()
    weights, stats = [], []
    for h in range(KEY_VALUE_HEADS):
        part = slice(HEAD_DIMENSION * h, HEAD_DIMENSION * (h + 1))
        full = lax.dot_general(
            qs[block * h : block * (h + 1), :].astype(BF16),
            kbuf[:, part],
            (((1,), (1,)), ((), ())),
            preferred_element_type=F32,
        )
        score = full[:, :extent]
        for r in range(1, rows):
            score = jnp.where(row_id == r, full[:, extent * r : extent * (r + 1)], score)
        masked = jnp.where(usable, score * SCALE, -1e30)
        peak = jnp.max(masked, axis=1, keepdims=True).astype(BF16).astype(F32)
        weight = jnp.where(usable, jnp.exp(masked - peak), 0.0).astype(BF16)
        weights.append(weight)
        total = jnp.sum(weight.astype(F32), axis=1, keepdims=True)
        stats.append((peak, total))
    for copy in copies[rows:]:
        copy.wait()
    for h in range(KEY_VALUE_HEADS):
        part = slice(HEAD_DIMENSION * h, HEAD_DIMENSION * (h + 1))
        peak, total = stats[h]
        wide = jnp.concatenate(
            [jnp.where(row_id == r, weights[h].astype(F32), 0.0) for r in range(rows)], axis=1
        ).astype(BF16)
        numerator = jnp.dot(wide, vbuf[:, part], preferred_element_type=F32)
        value = numerator / jnp.where(total > 0.0, total, 1.0)
        high = total.astype(BF16).astype(F32)
        extra = jnp.where(
            lane == 0,
            peak,
            jnp.where(lane == 1, high, jnp.where(lane == 2, total - high, spread)),
        )
        msg_ref[block * h : block * (h + 1), :LANES] = value.astype(BF16)
        msg_ref[block * h : block * (h + 1), LANES:] = extra.astype(BF16)


def project_kernel(arr_ref, q_ref, lk_ref, lv_ref, w_ref, msg_ref, resid_ref, sc, ov, hs):
    ranks, per, _ = arr_ref.shape
    rows = q_ref.shape[0]
    own_heads = per // rows
    place = lax.axis_index("tok")
    for j in range(own_heads):
        head = place * own_heads + j
        mine = pl.ds(pl.multiple_of(head * HEAD_DIMENSION, HEAD_DIMENSION), HEAD_DIMENSION)
        shared = pl.ds(
            pl.multiple_of((head // GROUP) * HEAD_DIMENSION, HEAD_DIMENSION), HEAD_DIMENSION
        )
        product = q_ref[:, mine].astype(F32) * lk_ref[:, shared].astype(F32)
        sc[rows * j : rows * (j + 1), :] = jnp.broadcast_to(
            jnp.sum(product, axis=1, keepdims=True) * SCALE, (rows, LANES)
        )
        ov[rows * j : rows * (j + 1), :] = lv_ref[:, shared].astype(F32)
    own_score = sc[:, :1]
    stats = [arr_ref[b, :, LANES:].astype(F32) for b in range(ranks)]
    top = own_score
    for b in range(ranks):
        top = jnp.maximum(top, stats[b][:, 0:1])
    self_weight = jnp.exp(own_score - top)
    combined = self_weight * ov[...]
    below = self_weight
    for b in range(ranks):
        factor = (stats[b][:, 1:2] + stats[b][:, 2:3]) * jnp.exp(stats[b][:, 0:1] - top)
        combined = combined + factor * arr_ref[b, :, :LANES].astype(F32)
        below = below + factor
    hs[...] = combined / below
    heads = jnp.concatenate(
        [hs[rows * j : rows * (j + 1), :] for j in range(own_heads)], axis=1
    ).astype(BF16)
    out = jnp.dot(heads, w_ref[...], preferred_element_type=F32).astype(BF16)
    for b in range(ranks):
        msg_ref[b] = out
    for b in range(ranks):
        for j in range(own_heads):
            start = HALF * (b * own_heads + j)
            resid_ref[:, start : start + HALF] = stats[b][rows * j : rows * (j + 1), HALF:]


def norm_kernel(arr_ref, resid_ref, gain_ref, att_ref, normed_ref, held):
    total = arr_ref[0].astype(F32)
    for b in range(1, arr_ref.shape[0]):
        total = total + arr_ref[b].astype(F32)
    held[...] = total
    hidden = resid_ref[...] + total
    scale = lax.rsqrt(jnp.sum(hidden * hidden, axis=1, keepdims=True) * (1.0 / D) + 1e-06)
    normed_ref[...] = (hidden * scale * gain_ref[...]).astype(BF16)
    width = att_ref.shape[1]
    if width % LANES == 0:
        start = pl.multiple_of(lax.axis_index("tok") * width, LANES)
        att_ref[...] = held[:, pl.ds(start, width)]
    else:
        place = lax.axis_index("tok")
        for b in range(D // width):
            @pl.when(place == b)
            def _():
                att_ref[...] = held[:, b * width : (b + 1) * width]


def expert_kernel(ids_ref, gates_ref, *refs, ranks, packed):
    sources = refs[:ranks]
    wg_ref, wu_ref, wd_ref, out_ref, lhs = refs[ranks:]
    subs, _, rows, _ = ids_ref.shape
    for k in range(ranks):
        lhs[rows * k : rows * (k + 1), :] = sources[k][...].astype(F32)
    x = lhs[...].astype(BF16)
    gate = jnp.dot(x, wg_ref[0], preferred_element_type=F32)
    up = jnp.dot(x, wu_ref[0], preferred_element_type=F32)
    act = (gate / (1.0 + jnp.exp(-gate)) * up).astype(BF16)
    y = jnp.dot(act, wd_ref[0], preferred_element_type=F32)
    mine = lax.axis_index("tok") * subs + lax.axis_index("sub")
    for k in range(ranks):
        e = lax.axis_index("exp") ^ (k // subs)
        s = lax.axis_index("sub") ^ (k % subs)
        named = jnp.where(ids_ref[s, e] == mine, gates_ref[s, e], 0.0)
        lhs[rows * k : rows * (k + 1), :] = y[rows * k : rows * (k + 1), :] * jnp.sum(
            named, axis=1, keepdims=True
        )
    if not packed:
        out_ref[...] = lhs[...].astype(BF16)
        return
    half = ranks * rows // 2
    left = lax.broadcasted_iota(jnp.int32, (half, LANES), 1) < HALF
    for c in range(D // LANES):
        upper = lhs[:half, LANES * c : LANES * (c + 1)]
        lower = lhs[half:, LANES * c : LANES * (c + 1)]
        out_ref[2 * c] = jnp.where(left, upper, pltpu.roll(lower, HALF, 1)).astype(BF16)
        out_ref[2 * c + 1] = jnp.where(left, pltpu.roll(upper, HALF, 1), lower).astype(BF16)


def mix_kernel(arr_ref, out_ref):
    subs, exps, rows, _ = out_ref.shape
    ranks = subs * exps
    half = ranks * rows // 2
    totals = []
    for g in range(ranks):
        total = arr_ref[g].astype(F32)
        for b in range(g + ranks, arr_ref.shape[0], ranks):
            total = total + arr_ref[b].astype(F32)
        totals.append(total)
    for j in range(ranks):
        mixed = None
        for g in range(ranks):
            row = (j ^ g) * rows
            lanes = slice(0, HALF) if row < half else slice(HALF, LANES)
            piece = totals[g][row % half : row % half + rows, lanes]
            mixed = piece if mixed is None else mixed + piece
        out_ref[j % subs, j // subs] = mixed


VMEM_SPEC = pl.BlockSpec(memory_space=pltpu.VMEM)
SMEM_SPEC = pl.BlockSpec(memory_space=pltpu.SMEM)
ANY_SPEC = pl.BlockSpec(memory_space=pl.ANY)


def call(kernel, shapes, in_specs, scratch, name, limit=None):
    many = isinstance(shapes, (list, tuple))
    return pl.pallas_call(
        kernel,
        out_shape=shapes,
        in_specs=in_specs,
        out_specs=[VMEM_SPEC] * len(shapes) if many else VMEM_SPEC,
        scratch_shapes=scratch,
        name=name,
        compiler_params=pltpu.CompilerParams(vmem_limit_bytes=limit),
    )


def body(
    query,
    key_cache_table,
    value_cache_table,
    latest_key,
    latest_value,
    lengths,
    resid,
    norm_gain,
    out_weight,
    expert_ids,
    gate_weights,
    w_gate,
    w_up,
    w_down,
):
    tok_ranks = lax.axis_size("tok")
    exp_ranks = lax.axis_size("exp")
    sub_ranks = lax.axis_size("sub")
    rows = query.shape[2]
    extent = key_cache_table.shape[3]
    feature_cols = resid.shape[3]
    own_heads = QUERY_HEADS // tok_ranks
    per = own_heads * rows
    keys = key_cache_table.reshape(rows, extent, KEY_VALUE_HEADS * HEAD_DIMENSION)
    values = value_cache_table.reshape(rows, extent, KEY_VALUE_HEADS * HEAD_DIMENSION)
    q = query.reshape(rows, QUERY_HEADS * HEAD_DIMENSION)
    message = call(
        attend_kernel,
        jax.ShapeDtypeStruct((QUERY_HEADS * rows, 2 * LANES), BF16),
        [SMEM_SPEC, VMEM_SPEC, VMEM_SPEC, ANY_SPEC, ANY_SPEC],
        [
            pltpu.VMEM((rows * extent, KEY_VALUE_HEADS * HEAD_DIMENSION), BF16),
            pltpu.VMEM((rows * extent, KEY_VALUE_HEADS * HEAD_DIMENSION), BF16),
            pltpu.VMEM((QUERY_HEADS * rows, HEAD_DIMENSION), F32),
            pltpu.VMEM((per, LANES), F32),
            pltpu.SemaphoreType.DMA((2, rows)),
        ],
        "attend",
    )(lengths, q, resid.reshape(rows, feature_cols), keys, values)
    arrived = lax.all_to_all(
        message.reshape(tok_ranks, per, 2 * LANES), "tok", split_axis=0, concat_axis=0, tiled=True
    )
    share, resid_full = call(
        project_kernel,
        [
            jax.ShapeDtypeStruct((tok_ranks, rows, D), BF16),
            jax.ShapeDtypeStruct((rows, D), F32),
        ],
        [VMEM_SPEC] * 5,
        [pltpu.VMEM((per, LANES), F32)] * 3,
        "project",
    )(
        arrived,
        q,
        latest_key.reshape(rows, KEY_VALUE_HEADS * HEAD_DIMENSION),
        latest_value.reshape(rows, KEY_VALUE_HEADS * HEAD_DIMENSION),
        out_weight,
    )
    shares = lax.all_to_all(share, "tok", split_axis=0, concat_axis=0, tiled=True)
    attended, normed = call(
        norm_kernel,
        [
            jax.ShapeDtypeStruct((rows, feature_cols), F32),
            jax.ShapeDtypeStruct((rows, D), BF16),
        ],
        [VMEM_SPEC] * 3,
        [pltpu.VMEM((rows, D), F32)],
        "norm",
    )(shares, resid_full, norm_gain.reshape(1, D))
    ranks = exp_ranks * sub_ranks
    pieces = [normed] + [
        lax.ppermute(normed, ("exp", "sub"), [(i, i ^ k) for i in range(ranks)])
        for k in range(1, ranks)
    ]
    block_cols = D // (tok_ranks * ranks)
    packed = 2 * block_cols == LANES
    rows_all = ranks * rows
    shape = (tok_ranks * ranks, rows_all // 2, LANES) if packed else (rows_all, D)
    weighted = call(
        functools.partial(expert_kernel, ranks=ranks, packed=packed),
        jax.ShapeDtypeStruct(shape, BF16),
        [VMEM_SPEC] * (5 + ranks),
        [pltpu.VMEM((rows_all, D), F32)],
        "experts",
    )(expert_ids, gate_weights, *pieces, w_gate, w_up, w_down)
    everywhere = ("tok", "exp", "sub")
    if packed:
        received = lax.all_to_all(weighted, everywhere, split_axis=0, concat_axis=0, tiled=True)
        expert_mix = call(
            mix_kernel,
            jax.ShapeDtypeStruct((sub_ranks, exp_ranks, rows, block_cols), F32),
            [VMEM_SPEC],
            [],
            "mix",
        )(received)
    else:
        blocks = jnp.transpose(weighted.reshape(rows_all, tok_ranks * ranks, block_cols), (1, 0, 2))
        received = lax.all_to_all(blocks, everywhere, split_axis=0, concat_axis=0, tiled=True)
        grouped = jnp.sum(
            received.astype(F32).reshape(tok_ranks, ranks, ranks, rows, block_cols), axis=0
        )
        mixed = [sum(grouped[g, j ^ g] for g in range(ranks)) for j in range(ranks)]
        expert_mix = jnp.transpose(
            jnp.stack(mixed).reshape(exp_ranks, sub_ranks, rows, block_cols), (1, 0, 2, 3)
        )
    return (attended.reshape(1, 1, rows, feature_cols), expert_mix)


def solution(mesh):
    placed = (
        P(("groups", "sub"), "exp", None, None),
        P(("groups", "sub"), "exp", None, "tok", None),
        P(("groups", "sub"), "exp", None, "tok", None),
        P(("groups", "sub"), "exp", None, None),
        P(("groups", "sub"), "exp", None, None),
        P(("groups", "sub"), "exp", None),
        P(("groups", "sub"), "exp", None, "tok"),
        P(),
        P("tok", None),
        P("groups", None, None, None),
        P("groups", None, None, None),
        P(("tok", "sub"), None, "exp"),
        P(("tok", "sub"), None, "exp"),
        P(("tok", "sub"), "exp", None),
    )
    return jax.shard_map(
        body,
        mesh=mesh,
        in_specs=placed,
        out_specs=(
            P(("groups", "sub"), "exp", None, "tok"),
            P("groups", None, None, ("tok", "exp", "sub")),
        ),
        check_vma=False,
    )
```

```python
import functools

import jax
import jax.numpy as jnp
from jax import lax
from jax.experimental import pallas as pl
from jax.experimental.pallas import tpu as pltpu
from jax.sharding import PartitionSpec as P

D = 2048
QUERY_HEADS = 32
KEY_VALUE_HEADS = 4
HEAD_DIMENSION = 128
TOPK = 8
GROUP = QUERY_HEADS // KEY_VALUE_HEADS
SCALE = HEAD_DIMENSION ** (-0.5)
LANES = 128
HALF = 64

F32 = jnp.float32
BF16 = jnp.bfloat16


def attend_kernel(
    len_hbm,
    q_hbm,
    resid_hbm,
    lk_hbm,
    lv_hbm,
    k_hbm,
    v_hbm,
    msg_ref,
    own_ref,
    len_ref,
    q_ref,
    resid_ref,
    lk_ref,
    lv_ref,
    kbuf,
    vbuf,
    qs,
    tail,
    sems,
    few,
):
    rows = q_ref.shape[0]
    extent = k_hbm.shape[1]
    own_heads = resid_ref.shape[1] // HALF
    block = GROUP * rows
    copies = []
    small = (
        (q_hbm, q_ref),
        (len_hbm, len_ref),
        (resid_hbm, resid_ref),
        (lk_hbm, lk_ref),
        (lv_hbm, lv_ref),
    )
    early = [pltpu.make_async_copy(*pair, few.at[n]) for n, pair in enumerate(small)]
    for copy in early:
        copy.start()
    for which, (source, target) in enumerate(((k_hbm, kbuf), (v_hbm, vbuf))):
        for r in range(rows):
            copy = pltpu.make_async_copy(
                source.at[r], target.at[pl.ds(r * extent, extent)], sems.at[which, r]
            )
            copy.start()
            copies.append(copy)
    for copy in early:
        copy.wait()
    place = lax.axis_index("tok")
    for h in range(QUERY_HEADS):
        qs[rows * h : rows * (h + 1), :] = q_ref[
            :, HEAD_DIMENSION * h : HEAD_DIMENSION * (h + 1)
        ].astype(F32)
    for j in range(own_heads):
        head = place * own_heads + j
        mine = pl.ds(pl.multiple_of(head * HEAD_DIMENSION, HEAD_DIMENSION), HEAD_DIMENSION)
        shared = pl.ds(
            pl.multiple_of((head // GROUP) * HEAD_DIMENSION, HEAD_DIMENSION), HEAD_DIMENSION
        )
        product = q_ref[:, mine].astype(F32) * lk_ref[:, shared].astype(F32)
        own_ref[rows * j : rows * (j + 1), LANES:] = jnp.broadcast_to(
            jnp.sum(product, axis=1, keepdims=True) * SCALE, (rows, LANES)
        )
        own_ref[rows * j : rows * (j + 1), :LANES] = lv_ref[:, shared].astype(F32)
    tail[...] = jnp.zeros_like(tail)
    for j in range(own_heads):
        tail[rows * j : rows * (j + 1), HALF:LANES] = resid_ref[
            :, HALF * j : HALF * (j + 1)
        ].astype(F32)
    row_id = lax.rem(lax.broadcasted_iota(jnp.int32, (block, 1), 0), rows)
    limit = jnp.zeros((block, 1), jnp.int32)
    for r in range(rows):
        limit = jnp.where(row_id == r, len_ref[0, 0, r], limit)
    first = place * extent
    usable = first + lax.broadcasted_iota(jnp.int32, (block, extent), 1) < limit
    lane = lax.broadcasted_iota(jnp.int32, (block, LANES), 1)
    per = own_heads * rows
    spread = jnp.concatenate([tail[...]] * (block // per), axis=0)
    for copy in copies[:rows]:
        copy.wait()
    weights, stats = [], []
    for h in range(KEY_VALUE_HEADS):
        part = slice(HEAD_DIMENSION * h, HEAD_DIMENSION * (h + 1))
        full = lax.dot_general(
            qs[block * h : block * (h + 1), :].astype(BF16),
            kbuf[:, part],
            (((1,), (1,)), ((), ())),
            preferred_element_type=F32,
        )
        score = full[:, :extent]
        for r in range(1, rows):
            score = jnp.where(row_id == r, full[:, extent * r : extent * (r + 1)], score)
        masked = jnp.where(usable, score * SCALE, -1e30)
        peak = jnp.max(masked, axis=1, keepdims=True).astype(BF16).astype(F32)
        weight = jnp.where(usable, jnp.exp(masked - peak), 0.0).astype(BF16)
        weights.append(weight)
        total = jnp.sum(weight.astype(F32), axis=1, keepdims=True)
        stats.append((peak, total))
    for copy in copies[rows:]:
        copy.wait()
    for h in range(KEY_VALUE_HEADS):
        part = slice(HEAD_DIMENSION * h, HEAD_DIMENSION * (h + 1))
        peak, total = stats[h]
        wide = jnp.concatenate(
            [jnp.where(row_id == r, weights[h].astype(F32), 0.0) for r in range(rows)], axis=1
        ).astype(BF16)
        numerator = jnp.dot(wide, vbuf[:, part], preferred_element_type=F32)
        value = numerator / jnp.where(total > 0.0, total, 1.0)
        high = total.astype(BF16).astype(F32)
        extra = jnp.where(
            lane == 0,
            peak,
            jnp.where(lane == 1, high, jnp.where(lane == 2, total - high, spread)),
        )
        msg_ref[block * h : block * (h + 1), :LANES] = value.astype(BF16)
        msg_ref[block * h : block * (h + 1), LANES:] = extra.astype(BF16)


def project_kernel(arr_ref, own_ref, w_ref, msg_ref, resid_ref, hs):
    ranks, per, _ = arr_ref.shape
    rows = resid_ref.shape[0]
    own_heads = per // rows
    own_score = own_ref[:, LANES : LANES + 1]
    stats = [arr_ref[b, :, LANES:].astype(F32) for b in range(ranks)]
    top = own_score
    for b in range(ranks):
        top = jnp.maximum(top, stats[b][:, 0:1])
    self_weight = jnp.exp(own_score - top)
    combined = self_weight * own_ref[:, :LANES]
    below = self_weight
    for b in range(ranks):
        factor = (stats[b][:, 1:2] + stats[b][:, 2:3]) * jnp.exp(stats[b][:, 0:1] - top)
        combined = combined + factor * arr_ref[b, :, :LANES].astype(F32)
        below = below + factor
    hs[...] = combined / below
    heads = jnp.concatenate(
        [hs[rows * j : rows * (j + 1), :] for j in range(own_heads)], axis=1
    ).astype(BF16)
    out = jnp.dot(heads, w_ref[...], preferred_element_type=F32).astype(BF16)
    for b in range(ranks):
        msg_ref[b] = out
    for b in range(ranks):
        for j in range(own_heads):
            start = HALF * (b * own_heads + j)
            resid_ref[:, start : start + HALF] = stats[b][rows * j : rows * (j + 1), HALF:]


def norm_kernel(arr_ref, resid_ref, gain_ref, att_ref, normed_ref, held):
    total = arr_ref[0].astype(F32)
    for b in range(1, arr_ref.shape[0]):
        total = total + arr_ref[b].astype(F32)
    held[...] = total
    hidden = resid_ref[...] + total
    scale = lax.rsqrt(jnp.sum(hidden * hidden, axis=1, keepdims=True) * (1.0 / D) + 1e-06)
    normed_ref[...] = (hidden * scale * gain_ref[...]).astype(BF16)
    width = att_ref.shape[1]
    if width % LANES == 0:
        start = pl.multiple_of(lax.axis_index("tok") * width, LANES)
        att_ref[...] = held[:, pl.ds(start, width)]
    else:
        place = lax.axis_index("tok")
        for b in range(D // width):
            @pl.when(place == b)
            def _():
                att_ref[...] = held[:, b * width : (b + 1) * width]


def expert_kernel(ids_ref, gates_ref, *refs, ranks, packed):
    sources = refs[:ranks]
    wg_ref, wu_ref, wd_ref, out_ref, lhs = refs[ranks:]
    subs, _, rows, _ = ids_ref.shape
    for k in range(ranks):
        lhs[rows * k : rows * (k + 1), :] = sources[k][...].astype(F32)
    x = lhs[...].astype(BF16)
    gate = jnp.dot(x, wg_ref[0], preferred_element_type=F32)
    up = jnp.dot(x, wu_ref[0], preferred_element_type=F32)
    act = (gate / (1.0 + jnp.exp(-gate)) * up).astype(BF16)
    y = jnp.dot(act, wd_ref[0], preferred_element_type=F32)
    mine = lax.axis_index("tok") * subs + lax.axis_index("sub")
    for k in range(ranks):
        e = lax.axis_index("exp") ^ (k // subs)
        s = lax.axis_index("sub") ^ (k % subs)
        named = jnp.where(ids_ref[s, e] == mine, gates_ref[s, e], 0.0)
        lhs[rows * k : rows * (k + 1), :] = y[rows * k : rows * (k + 1), :] * jnp.sum(
            named, axis=1, keepdims=True
        )
    if not packed:
        out_ref[...] = lhs[...].astype(BF16)
        return
    half = ranks * rows // 2
    left = lax.broadcasted_iota(jnp.int32, (half, LANES), 1) < HALF
    for c in range(D // LANES):
        upper = lhs[:half, LANES * c : LANES * (c + 1)]
        lower = lhs[half:, LANES * c : LANES * (c + 1)]
        out_ref[2 * c] = jnp.where(left, upper, pltpu.roll(lower, HALF, 1)).astype(BF16)
        out_ref[2 * c + 1] = jnp.where(left, pltpu.roll(upper, HALF, 1), lower).astype(BF16)


def mix_kernel(arr_ref, out_ref):
    subs, exps, rows, _ = out_ref.shape
    ranks = subs * exps
    half = ranks * rows // 2
    totals = []
    for g in range(ranks):
        total = arr_ref[g].astype(F32)
        for b in range(g + ranks, arr_ref.shape[0], ranks):
            total = total + arr_ref[b].astype(F32)
        totals.append(total)
    for j in range(ranks):
        mixed = None
        for g in range(ranks):
            row = (j ^ g) * rows
            lanes = slice(0, HALF) if row < half else slice(HALF, LANES)
            piece = totals[g][row % half : row % half + rows, lanes]
            mixed = piece if mixed is None else mixed + piece
        out_ref[j % subs, j // subs] = mixed


VMEM_SPEC = pl.BlockSpec(memory_space=pltpu.VMEM)
HBM_SPEC = pl.BlockSpec(memory_space=pltpu.HBM)


def call(kernel, shapes, in_specs, scratch, name, cost=0, limit=8 * 1024 * 1024):
    many = isinstance(shapes, (list, tuple))
    return pl.pallas_call(
        kernel,
        out_shape=shapes,
        in_specs=in_specs,
        out_specs=[VMEM_SPEC] * len(shapes) if many else VMEM_SPEC,
        scratch_shapes=scratch,
        name=name,
        cost_estimate=pl.CostEstimate(flops=cost, bytes_accessed=cost // 700, transcendentals=0),
        compiler_params=pltpu.CompilerParams(vmem_limit_bytes=limit),
    )


def body(
    query,
    key_cache_table,
    value_cache_table,
    latest_key,
    latest_value,
    lengths,
    resid,
    norm_gain,
    out_weight,
    expert_ids,
    gate_weights,
    w_gate,
    w_up,
    w_down,
):
    tok_ranks = lax.axis_size("tok")
    exp_ranks = lax.axis_size("exp")
    sub_ranks = lax.axis_size("sub")
    rows = query.shape[2]
    extent = key_cache_table.shape[3]
    feature_cols = resid.shape[3]
    own_heads = QUERY_HEADS // tok_ranks
    per = own_heads * rows
    keys = key_cache_table.reshape(rows, extent, KEY_VALUE_HEADS * HEAD_DIMENSION)
    values = value_cache_table.reshape(rows, extent, KEY_VALUE_HEADS * HEAD_DIMENSION)
    q = query.reshape(rows, QUERY_HEADS * HEAD_DIMENSION)
    shared_cols = KEY_VALUE_HEADS * HEAD_DIMENSION
    message, own = call(
        attend_kernel,
        [
            jax.ShapeDtypeStruct((QUERY_HEADS * rows, 2 * LANES), BF16),
            jax.ShapeDtypeStruct((per, 2 * LANES), F32),
        ],
        [HBM_SPEC] * 7,
        [
            pltpu.SMEM(lengths.shape, jnp.int32),
            pltpu.VMEM((rows, QUERY_HEADS * HEAD_DIMENSION), BF16),
            pltpu.VMEM((rows, feature_cols), BF16),
            pltpu.VMEM((rows, shared_cols), BF16),
            pltpu.VMEM((rows, shared_cols), BF16),
            pltpu.VMEM((rows * extent, shared_cols), BF16),
            pltpu.VMEM((rows * extent, shared_cols), BF16),
            pltpu.VMEM((QUERY_HEADS * rows, HEAD_DIMENSION), F32),
            pltpu.VMEM((per, LANES), F32),
            pltpu.SemaphoreType.DMA((2, rows)),
            pltpu.SemaphoreType.DMA((5,)),
        ],
        "attend",
        cost=20_000_000_000,
    )(
        *(
            pltpu.with_memory_space_constraint(x, pltpu.HBM)
            for x in (
                lengths,
                q,
                resid.reshape(rows, feature_cols),
                latest_key.reshape(rows, shared_cols),
                latest_value.reshape(rows, shared_cols),
                keys,
                values,
            )
        )
    )
    arrived = lax.all_to_all(
        message.reshape(tok_ranks, per, 2 * LANES), "tok", split_axis=0, concat_axis=0, tiled=True
    )
    share, resid_full = call(
        project_kernel,
        [
            jax.ShapeDtypeStruct((tok_ranks, rows, D), BF16),
            jax.ShapeDtypeStruct((rows, D), F32),
        ],
        [VMEM_SPEC] * 3,
        [pltpu.VMEM((per, LANES), F32)],
        "project",
        cost=20_000_000_000,
    )(arrived, own, out_weight)
    shares = lax.all_to_all(share, "tok", split_axis=0, concat_axis=0, tiled=True)
    attended, normed = call(
        norm_kernel,
        [
            jax.ShapeDtypeStruct((rows, feature_cols), F32),
            jax.ShapeDtypeStruct((rows, D), BF16),
        ],
        [VMEM_SPEC] * 3,
        [pltpu.VMEM((rows, D), F32)],
        "norm",
        cost=20_000_000_000,
    )(shares, resid_full, norm_gain.reshape(1, D))
    ranks = exp_ranks * sub_ranks
    pieces = [normed] + [
        lax.ppermute(normed, ("exp", "sub"), [(i, i ^ k) for i in range(ranks)])
        for k in range(1, ranks)
    ]
    block_cols = D // (tok_ranks * ranks)
    packed = 2 * block_cols == LANES
    rows_all = ranks * rows
    shape = (tok_ranks * ranks, rows_all // 2, LANES) if packed else (rows_all, D)
    weighted = call(
        functools.partial(expert_kernel, ranks=ranks, packed=packed),
        jax.ShapeDtypeStruct(shape, BF16),
        [VMEM_SPEC] * (5 + ranks),
        [pltpu.VMEM((rows_all, D), F32)],
        "experts",
    )(expert_ids, gate_weights, *pieces, w_gate, w_up, w_down)
    everywhere = ("tok", "exp", "sub")
    if packed:
        received = lax.all_to_all(weighted, everywhere, split_axis=0, concat_axis=0, tiled=True)
        expert_mix = call(
            mix_kernel,
            jax.ShapeDtypeStruct((sub_ranks, exp_ranks, rows, block_cols), F32),
            [VMEM_SPEC],
            [],
            "mix",
        )(received)
    else:
        blocks = jnp.transpose(weighted.reshape(rows_all, tok_ranks * ranks, block_cols), (1, 0, 2))
        received = lax.all_to_all(blocks, everywhere, split_axis=0, concat_axis=0, tiled=True)
        grouped = jnp.sum(
            received.astype(F32).reshape(tok_ranks, ranks, ranks, rows, block_cols), axis=0
        )
        mixed = [sum(grouped[g, j ^ g] for g in range(ranks)) for j in range(ranks)]
        expert_mix = jnp.transpose(
            jnp.stack(mixed).reshape(exp_ranks, sub_ranks, rows, block_cols), (1, 0, 2, 3)
        )
    return (attended.reshape(1, 1, rows, feature_cols), expert_mix)


def solution(mesh):
    placed = (
        P(("groups", "sub"), "exp", None, None),
        P(("groups", "sub"), "exp", None, "tok", None),
        P(("groups", "sub"), "exp", None, "tok", None),
        P(("groups", "sub"), "exp", None, None),
        P(("groups", "sub"), "exp", None, None),
        P(("groups", "sub"), "exp", None),
        P(("groups", "sub"), "exp", None, "tok"),
        P(),
        P("tok", None),
        P("groups", None, None, None),
        P("groups", None, None, None),
        P(("tok", "sub"), None, "exp"),
        P(("tok", "sub"), None, "exp"),
        P(("tok", "sub"), "exp", None),
    )
    return jax.shard_map(
        body,
        mesh=mesh,
        in_specs=placed,
        out_specs=(
            P(("groups", "sub"), "exp", None, "tok"),
            P("groups", None, None, ("tok", "exp", "sub")),
        ),
        check_vma=False,
    )
```

```python
import functools

import jax
import jax.numpy as jnp
from jax import lax
from jax.experimental import pallas as pl
from jax.experimental.pallas import tpu as pltpu
from jax.sharding import PartitionSpec as P

D = 2048
QUERY_HEADS = 32
KEY_VALUE_HEADS = 4
HEAD_DIMENSION = 128
TOPK = 8
GROUP = QUERY_HEADS // KEY_VALUE_HEADS
SCALE = HEAD_DIMENSION ** (-0.5)
LANES = 128
HALF = 64

F32 = jnp.float32
BF16 = jnp.bfloat16


def attend_kernel(
    len_hbm,
    q_hbm,
    lk_hbm,
    lv_hbm,
    k_hbm,
    v_hbm,
    msg_ref,
    own_ref,
    len_ref,
    q_ref,
    lk_ref,
    lv_ref,
    kbuf,
    vbuf,
    qs,
    sems,
    few,
):
    rows = q_ref.shape[0]
    extent = k_hbm.shape[1]
    own_heads = own_ref.shape[0] // rows
    block = GROUP * rows
    copies = []
    small = (
        (q_hbm, q_ref),
        (len_hbm, len_ref),
        (lk_hbm, lk_ref),
        (lv_hbm, lv_ref),
    )
    early = [pltpu.make_async_copy(*pair, few.at[n]) for n, pair in enumerate(small)]
    for copy in early:
        copy.start()
    for which, (source, target) in enumerate(((k_hbm, kbuf), (v_hbm, vbuf))):
        for r in range(rows):
            copy = pltpu.make_async_copy(
                source.at[r], target.at[pl.ds(r * extent, extent)], sems.at[which, r]
            )
            copy.start()
            copies.append(copy)
    for copy in early:
        copy.wait()
    place = lax.axis_index("tok")
    for h in range(QUERY_HEADS):
        qs[rows * h : rows * (h + 1), :] = q_ref[
            :, HEAD_DIMENSION * h : HEAD_DIMENSION * (h + 1)
        ].astype(F32)
    for j in range(own_heads):
        head = place * own_heads + j
        mine = pl.ds(pl.multiple_of(head * HEAD_DIMENSION, HEAD_DIMENSION), HEAD_DIMENSION)
        shared = pl.ds(
            pl.multiple_of((head // GROUP) * HEAD_DIMENSION, HEAD_DIMENSION), HEAD_DIMENSION
        )
        product = q_ref[:, mine].astype(F32) * lk_ref[:, shared].astype(F32)
        own_ref[rows * j : rows * (j + 1), LANES:] = jnp.broadcast_to(
            jnp.sum(product, axis=1, keepdims=True) * SCALE, (rows, LANES)
        )
        own_ref[rows * j : rows * (j + 1), :LANES] = lv_ref[:, shared].astype(F32)
    row_id = lax.rem(lax.broadcasted_iota(jnp.int32, (block, 1), 0), rows)
    limit = jnp.zeros((block, 1), jnp.int32)
    for r in range(rows):
        limit = jnp.where(row_id == r, len_ref[0, 0, r], limit)
    first = place * extent
    usable = first + lax.broadcasted_iota(jnp.int32, (block, extent), 1) < limit
    lane = lax.broadcasted_iota(jnp.int32, (block, LANES), 1)
    for copy in copies[:rows]:
        copy.wait()
    weights, stats = [], []
    for h in range(KEY_VALUE_HEADS):
        part = slice(HEAD_DIMENSION * h, HEAD_DIMENSION * (h + 1))
        full = lax.dot_general(
            qs[block * h : block * (h + 1), :].astype(BF16),
            kbuf[:, part],
            (((1,), (1,)), ((), ())),
            preferred_element_type=F32,
        )
        score = full[:, :extent]
        for r in range(1, rows):
            score = jnp.where(row_id == r, full[:, extent * r : extent * (r + 1)], score)
        masked = jnp.where(usable, score * SCALE, -1e30)
        peak = jnp.max(masked, axis=1, keepdims=True).astype(BF16).astype(F32)
        weight = jnp.where(usable, jnp.exp(masked - peak), 0.0).astype(BF16)
        weights.append(weight)
        total = jnp.sum(weight.astype(F32), axis=1, keepdims=True)
        stats.append((peak, total))
    for copy in copies[rows:]:
        copy.wait()
    for h in range(KEY_VALUE_HEADS):
        part = slice(HEAD_DIMENSION * h, HEAD_DIMENSION * (h + 1))
        peak, total = stats[h]
        wide = jnp.concatenate(
            [jnp.where(row_id == r, weights[h].astype(F32), 0.0) for r in range(rows)], axis=1
        ).astype(BF16)
        numerator = jnp.dot(wide, vbuf[:, part], preferred_element_type=F32)
        value = numerator / jnp.where(total > 0.0, total, 1.0)
        high = total.astype(BF16).astype(F32)
        extra = jnp.where(lane == 0, peak, jnp.where(lane == 1, high, total - high))
        msg_ref[block * h : block * (h + 1), :LANES] = value.astype(BF16)
        msg_ref[block * h : block * (h + 1), LANES:] = extra.astype(BF16)


def project_kernel(arr_ref, own_ref, mine_ref, w_ref, msg_ref, raw_ref, hs, held):
    ranks, per, _ = arr_ref.shape
    rows, width = mine_ref.shape
    own_heads = per // rows
    own_score = own_ref[:, LANES : LANES + 1]
    stats = [arr_ref[b, :, LANES:].astype(F32) for b in range(ranks)]
    top = own_score
    for b in range(ranks):
        top = jnp.maximum(top, stats[b][:, 0:1])
    self_weight = jnp.exp(own_score - top)
    combined = self_weight * own_ref[:, :LANES]
    below = self_weight
    for b in range(ranks):
        factor = (stats[b][:, 1:2] + stats[b][:, 2:3]) * jnp.exp(stats[b][:, 0:1] - top)
        combined = combined + factor * arr_ref[b, :, :LANES].astype(F32)
        below = below + factor
    hs[...] = combined / below
    heads = jnp.concatenate(
        [hs[rows * j : rows * (j + 1), :] for j in range(own_heads)], axis=1
    ).astype(BF16)
    out = jnp.dot(heads, w_ref[...], preferred_element_type=F32)
    held[...] = out
    place = lax.axis_index("tok")
    if width % LANES == 0:
        slot = pl.ds(pl.multiple_of(place * width, LANES), width)
        raw_ref[...] = held[:, slot]
        held[:, slot] = raw_ref[...] + mine_ref[...].astype(F32)
    else:
        for b in range(ranks):

            @pl.when(place == b)
            def _():
                slot = slice(b * width, (b + 1) * width)
                raw_ref[...] = held[:, slot]
                held[:, slot] = raw_ref[...] + mine_ref[...].astype(F32)

    sent = held[...].astype(BF16)
    for b in range(msg_ref.shape[0]):
        msg_ref[b] = sent


def norm_kernel(arr_ref, raw_ref, gain_ref, att_ref, normed_ref):
    exps = normed_ref.shape[0]
    ranks = arr_ref.shape[0] // exps
    for k in range(exps):
        source = lax.axis_index("exp") ^ k
        hidden = arr_ref[source].astype(F32)
        for b in range(1, ranks):
            hidden = hidden + arr_ref[source + b * exps].astype(F32)
        scale = lax.rsqrt(jnp.sum(hidden * hidden, axis=1, keepdims=True) * (1.0 / D) + 1e-06)
        normed_ref[k] = (hidden * scale * gain_ref[...]).astype(BF16)
    width = att_ref.shape[1]
    place = lax.axis_index("tok")
    mine = lax.axis_index("exp")

    def gather(slot):
        total = raw_ref[...]
        for b in range(ranks):
            part = arr_ref[mine + b * exps, :, slot].astype(F32)
            total = total + jnp.where(place == b, 0.0, part)
        att_ref[...] = total

    if width % LANES == 0:
        gather(pl.ds(pl.multiple_of(place * width, LANES), width))
    else:
        for b in range(ranks):
            pl.when(place == b)(functools.partial(gather, slice(b * width, (b + 1) * width)))


def expert_kernel(ids_ref, gates_ref, *refs, ranks, packed):
    subs, exps, rows, _ = ids_ref.shape
    sources = refs[:subs]
    wg_ref, wu_ref, wd_ref, out_ref, lhs = refs[subs:]
    for k in range(ranks):
        lhs[rows * k : rows * (k + 1), :] = sources[k % subs][k // subs].astype(F32)
    x = lhs[...].astype(BF16)
    gate = jnp.dot(x, wg_ref[0], preferred_element_type=F32)
    up = jnp.dot(x, wu_ref[0], preferred_element_type=F32)
    act = (gate / (1.0 + jnp.exp(-gate)) * up).astype(BF16)
    y = jnp.dot(act, wd_ref[0], preferred_element_type=F32)
    mine = lax.axis_index("tok") * subs + lax.axis_index("sub")
    for k in range(ranks):
        e = lax.axis_index("exp") ^ (k // subs)
        s = lax.axis_index("sub") ^ (k % subs)
        named = jnp.where(ids_ref[s, e] == mine, gates_ref[s, e], 0.0)
        lhs[rows * k : rows * (k + 1), :] = y[rows * k : rows * (k + 1), :] * jnp.sum(
            named, axis=1, keepdims=True
        )
    if not packed:
        out_ref[...] = lhs[...].astype(BF16)
        return
    half = ranks * rows // 2
    left = lax.broadcasted_iota(jnp.int32, (half, LANES), 1) < HALF
    for c in range(D // LANES):
        upper = lhs[:half, LANES * c : LANES * (c + 1)]
        lower = lhs[half:, LANES * c : LANES * (c + 1)]
        out_ref[2 * c] = jnp.where(left, upper, pltpu.roll(lower, HALF, 1)).astype(BF16)
        out_ref[2 * c + 1] = jnp.where(left, pltpu.roll(upper, HALF, 1), lower).astype(BF16)


def mix_kernel(arr_ref, att_ref, out_ref, final_ref):
    final_ref[...] = att_ref[...]
    subs, exps, rows, _ = out_ref.shape
    ranks = subs * exps
    half = ranks * rows // 2
    totals = []
    for g in range(ranks):
        total = arr_ref[g].astype(F32)
        for b in range(g + ranks, arr_ref.shape[0], ranks):
            total = total + arr_ref[b].astype(F32)
        totals.append(total)
    for j in range(ranks):
        mixed = None
        for g in range(ranks):
            row = (j ^ g) * rows
            lanes = slice(0, HALF) if row < half else slice(HALF, LANES)
            piece = totals[g][row % half : row % half + rows, lanes]
            mixed = piece if mixed is None else mixed + piece
        out_ref[j % subs, j // subs] = mixed


VMEM_SPEC = pl.BlockSpec(memory_space=pltpu.VMEM)
HBM_SPEC = pl.BlockSpec(memory_space=pltpu.HBM)


def call(kernel, shapes, in_specs, scratch, name, cost=0, limit=8 * 1024 * 1024):
    many = isinstance(shapes, (list, tuple))
    return pl.pallas_call(
        kernel,
        out_shape=shapes,
        in_specs=in_specs,
        out_specs=[VMEM_SPEC] * len(shapes) if many else VMEM_SPEC,
        scratch_shapes=scratch,
        name=name,
        cost_estimate=pl.CostEstimate(flops=cost, bytes_accessed=cost // 700, transcendentals=0),
        compiler_params=pltpu.CompilerParams(vmem_limit_bytes=limit),
    )


def body(
    query,
    key_cache_table,
    value_cache_table,
    latest_key,
    latest_value,
    lengths,
    resid,
    norm_gain,
    out_weight,
    expert_ids,
    gate_weights,
    w_gate,
    w_up,
    w_down,
):
    tok_ranks = lax.axis_size("tok")
    exp_ranks = lax.axis_size("exp")
    sub_ranks = lax.axis_size("sub")
    rows = query.shape[2]
    extent = key_cache_table.shape[3]
    feature_cols = resid.shape[3]
    own_heads = QUERY_HEADS // tok_ranks
    per = own_heads * rows
    keys = key_cache_table.reshape(rows, extent, KEY_VALUE_HEADS * HEAD_DIMENSION)
    values = value_cache_table.reshape(rows, extent, KEY_VALUE_HEADS * HEAD_DIMENSION)
    q = query.reshape(rows, QUERY_HEADS * HEAD_DIMENSION)
    shared_cols = KEY_VALUE_HEADS * HEAD_DIMENSION
    message, own = call(
        attend_kernel,
        [
            jax.ShapeDtypeStruct((QUERY_HEADS * rows, 2 * LANES), BF16),
            jax.ShapeDtypeStruct((per, 2 * LANES), F32),
        ],
        [HBM_SPEC] * 6,
        [
            pltpu.SMEM(lengths.shape, jnp.int32),
            pltpu.VMEM((rows, QUERY_HEADS * HEAD_DIMENSION), BF16),
            pltpu.VMEM((rows, shared_cols), BF16),
            pltpu.VMEM((rows, shared_cols), BF16),
            pltpu.VMEM((rows * extent, shared_cols), BF16),
            pltpu.VMEM((rows * extent, shared_cols), BF16),
            pltpu.VMEM((QUERY_HEADS * rows, HEAD_DIMENSION), F32),
            pltpu.SemaphoreType.DMA((2, rows)),
            pltpu.SemaphoreType.DMA((4,)),
        ],
        "attend",
        cost=20_000_000_000,
    )(
        *(
            pltpu.with_memory_space_constraint(x, pltpu.HBM)
            for x in (
                lengths,
                q,
                latest_key.reshape(rows, shared_cols),
                latest_value.reshape(rows, shared_cols),
                keys,
                values,
            )
        )
    )
    arrived = lax.all_to_all(
        message.reshape(tok_ranks, per, 2 * LANES), "tok", split_axis=0, concat_axis=0, tiled=True
    )
    share, raw = call(
        project_kernel,
        [
            jax.ShapeDtypeStruct((tok_ranks * exp_ranks, rows, D), BF16),
            jax.ShapeDtypeStruct((rows, feature_cols), F32),
        ],
        [VMEM_SPEC] * 4,
        [pltpu.VMEM((per, LANES), F32), pltpu.VMEM((rows, D), F32)],
        "project",
        cost=20_000_000_000,
    )(arrived, own, resid.reshape(rows, feature_cols), out_weight)
    shares = lax.all_to_all(share, ("tok", "exp"), split_axis=0, concat_axis=0, tiled=True)
    attended, normed = call(
        norm_kernel,
        [
            jax.ShapeDtypeStruct((rows, feature_cols), F32),
            jax.ShapeDtypeStruct((exp_ranks, rows, D), BF16),
        ],
        [VMEM_SPEC] * 3,
        [],
        "norm",
    )(shares, raw, norm_gain.reshape(1, D))
    ranks = exp_ranks * sub_ranks
    pieces = [normed] + [
        lax.ppermute(normed, "sub", [(i, i ^ k) for i in range(sub_ranks)])
        for k in range(1, sub_ranks)
    ]
    block_cols = D // (tok_ranks * ranks)
    packed = 2 * block_cols == LANES
    rows_all = ranks * rows
    shape = (tok_ranks * ranks, rows_all // 2, LANES) if packed else (rows_all, D)
    weighted = call(
        functools.partial(expert_kernel, ranks=ranks, packed=packed),
        jax.ShapeDtypeStruct(shape, BF16),
        [VMEM_SPEC] * (5 + sub_ranks),
        [pltpu.VMEM((rows_all, D), F32)],
        "experts",
    )(expert_ids, gate_weights, *pieces, w_gate, w_up, w_down)
    everywhere = ("tok", "exp", "sub")
    if packed:
        received = lax.all_to_all(weighted, everywhere, split_axis=0, concat_axis=0, tiled=True)
        expert_mix, attended = call(
            mix_kernel,
            [
                jax.ShapeDtypeStruct((sub_ranks, exp_ranks, rows, block_cols), F32),
                jax.ShapeDtypeStruct((rows, feature_cols), F32),
            ],
            [VMEM_SPEC] * 2,
            [],
            "mix",
        )(received, attended)
    else:
        blocks = jnp.transpose(weighted.reshape(rows_all, tok_ranks * ranks, block_cols), (1, 0, 2))
        received = lax.all_to_all(blocks, everywhere, split_axis=0, concat_axis=0, tiled=True)
        grouped = jnp.sum(
            received.astype(F32).reshape(tok_ranks, ranks, ranks, rows, block_cols), axis=0
        )
        mixed = [sum(grouped[g, j ^ g] for g in range(ranks)) for j in range(ranks)]
        expert_mix = jnp.transpose(
            jnp.stack(mixed).reshape(exp_ranks, sub_ranks, rows, block_cols), (1, 0, 2, 3)
        )
    return (attended.reshape(1, 1, rows, feature_cols), expert_mix)


def solution(mesh):
    placed = (
        P(("groups", "sub"), "exp", None, None),
        P(("groups", "sub"), "exp", None, "tok", None),
        P(("groups", "sub"), "exp", None, "tok", None),
        P(("groups", "sub"), "exp", None, None),
        P(("groups", "sub"), "exp", None, None),
        P(("groups", "sub"), "exp", None),
        P(("groups", "sub"), "exp", None, "tok"),
        P(),
        P("tok", None),
        P("groups", None, None, None),
        P("groups", None, None, None),
        P(("tok", "sub"), None, "exp"),
        P(("tok", "sub"), None, "exp"),
        P(("tok", "sub"), "exp", None),
    )
    return jax.shard_map(
        body,
        mesh=mesh,
        in_specs=placed,
        out_specs=(
            P(("groups", "sub"), "exp", None, "tok"),
            P("groups", None, None, ("tok", "exp", "sub")),
        ),
        check_vma=False,
    )
```

```python
import functools

import jax
import jax.numpy as jnp
from jax import lax
from jax.experimental import pallas as pl
from jax.experimental.pallas import tpu as pltpu
from jax.sharding import PartitionSpec as P

D = 2048
QUERY_HEADS = 32
KEY_VALUE_HEADS = 4
HEAD_DIMENSION = 128
TOPK = 8
GROUP = QUERY_HEADS // KEY_VALUE_HEADS
SCALE = HEAD_DIMENSION ** (-0.5)
LANES = 128
HALF = 64
PIECES = 8

F32 = jnp.float32
BF16 = jnp.bfloat16


def attend_kernel(
    len_hbm,
    q_hbm,
    lk_hbm,
    lv_hbm,
    k_hbm,
    v_hbm,
    msg_ref,
    own_ref,
    len_ref,
    q_ref,
    lk_ref,
    lv_ref,
    kbuf,
    vbuf,
    qs,
    sems,
):
    rows = q_ref.shape[0]
    extent = k_hbm.shape[1]
    own_heads = own_ref.shape[0] // rows
    block = GROUP * rows
    cut = extent // PIECES
    copies = [
        pltpu.make_async_copy(source, target, sems.at[0])
        for source, target in (
            (q_hbm, q_ref),
            (len_hbm, len_ref),
            (lk_hbm, lk_ref),
            (lv_hbm, lv_ref),
        )
    ]
    early = len(copies)
    for which, (source, target) in enumerate(((k_hbm, kbuf), (v_hbm, vbuf))):
        for r in range(rows):
            for c in range(PIECES):
                copies.append(
                    pltpu.make_async_copy(
                        source.at[r, pl.ds(cut * c, cut)],
                        target.at[pl.ds(r * extent + cut * c, cut)],
                        sems.at[1 + which],
                    )
                )
    middle = early + rows * PIECES
    for n, copy in enumerate(copies):
        copy.start(priority=1 if n >= middle else 0)
    for copy in copies[:early]:
        copy.wait()
    place = lax.axis_index("tok")
    for h in range(QUERY_HEADS):
        qs[rows * h : rows * (h + 1), :] = q_ref[
            :, HEAD_DIMENSION * h : HEAD_DIMENSION * (h + 1)
        ].astype(F32)
    for j in range(own_heads):
        head = place * own_heads + j
        mine = pl.ds(pl.multiple_of(head * HEAD_DIMENSION, HEAD_DIMENSION), HEAD_DIMENSION)
        shared = pl.ds(
            pl.multiple_of((head // GROUP) * HEAD_DIMENSION, HEAD_DIMENSION), HEAD_DIMENSION
        )
        product = q_ref[:, mine].astype(F32) * lk_ref[:, shared].astype(F32)
        own_ref[rows * j : rows * (j + 1), LANES:] = jnp.broadcast_to(
            jnp.sum(product, axis=1, keepdims=True) * SCALE, (rows, LANES)
        )
        own_ref[rows * j : rows * (j + 1), :LANES] = lv_ref[:, shared].astype(F32)
    row_id = lax.rem(lax.broadcasted_iota(jnp.int32, (block, 1), 0), rows)
    limit = jnp.zeros((block, 1), jnp.int32)
    for r in range(rows):
        limit = jnp.where(row_id == r, len_ref[0, 0, r], limit)
    first = place * extent
    usable = first + lax.broadcasted_iota(jnp.int32, (block, extent), 1) < limit
    lane = lax.broadcasted_iota(jnp.int32, (block, LANES), 1)
    for copy in copies[early:middle]:
        copy.wait()
    weights, stats = [], []
    for h in range(KEY_VALUE_HEADS):
        part = slice(HEAD_DIMENSION * h, HEAD_DIMENSION * (h + 1))
        full = lax.dot_general(
            qs[block * h : block * (h + 1), :].astype(BF16),
            kbuf[:, part],
            (((1,), (1,)), ((), ())),
            preferred_element_type=F32,
        )
        score = full[:, :extent]
        for r in range(1, rows):
            score = jnp.where(row_id == r, full[:, extent * r : extent * (r + 1)], score)
        masked = jnp.where(usable, score * SCALE, -1e30)
        peak = jnp.max(masked, axis=1, keepdims=True).astype(BF16).astype(F32)
        weight = jnp.where(usable, jnp.exp(masked - peak), 0.0).astype(BF16)
        weights.append(weight)
        total = jnp.sum(weight.astype(F32), axis=1, keepdims=True)
        stats.append((peak, total))
    for copy in copies[middle:]:
        copy.wait()
    for h in range(KEY_VALUE_HEADS):
        part = slice(HEAD_DIMENSION * h, HEAD_DIMENSION * (h + 1))
        peak, total = stats[h]
        wide = jnp.concatenate(
            [jnp.where(row_id == r, weights[h].astype(F32), 0.0) for r in range(rows)], axis=1
        ).astype(BF16)
        numerator = jnp.dot(wide, vbuf[:, part], preferred_element_type=F32)
        value = numerator / jnp.where(total > 0.0, total, 1.0)
        high = total.astype(BF16).astype(F32)
        extra = jnp.where(lane == 0, peak, jnp.where(lane == 1, high, total - high))
        msg_ref[block * h : block * (h + 1), :LANES] = value.astype(BF16)
        msg_ref[block * h : block * (h + 1), LANES:] = extra.astype(BF16)


def project_kernel(arr_ref, own_ref, mine_ref, w_ref, msg_ref, raw_ref, hs, held):
    ranks, per, _ = arr_ref.shape
    rows, width = mine_ref.shape
    own_heads = per // rows
    own_score = own_ref[:, LANES : LANES + 1]
    stats = [arr_ref[b, :, LANES:].astype(F32) for b in range(ranks)]
    top = own_score
    for b in range(ranks):
        top = jnp.maximum(top, stats[b][:, 0:1])
    self_weight = jnp.exp(own_score - top)
    combined = self_weight * own_ref[:, :LANES]
    below = self_weight
    for b in range(ranks):
        factor = (stats[b][:, 1:2] + stats[b][:, 2:3]) * jnp.exp(stats[b][:, 0:1] - top)
        combined = combined + factor * arr_ref[b, :, :LANES].astype(F32)
        below = below + factor
    hs[...] = combined / below
    heads = jnp.concatenate(
        [hs[rows * j : rows * (j + 1), :] for j in range(own_heads)], axis=1
    ).astype(BF16)
    out = jnp.dot(heads, w_ref[...], preferred_element_type=F32)
    held[...] = out
    place = lax.axis_index("tok")
    if width % LANES == 0:
        slot = pl.ds(pl.multiple_of(place * width, LANES), width)
        raw_ref[...] = held[:, slot]
        held[:, slot] = raw_ref[...] + mine_ref[...].astype(F32)
    else:
        for b in range(ranks):

            @pl.when(place == b)
            def _():
                slot = slice(b * width, (b + 1) * width)
                raw_ref[...] = held[:, slot]
                held[:, slot] = raw_ref[...] + mine_ref[...].astype(F32)

    sent = held[...].astype(BF16)
    for b in range(msg_ref.shape[0]):
        msg_ref[b] = sent


def norm_kernel(arr_ref, raw_ref, gain_ref, att_ref, normed_ref):
    exps = normed_ref.shape[0]
    ranks = arr_ref.shape[0] // exps
    for k in range(exps):
        source = lax.axis_index("exp") ^ k
        hidden = arr_ref[source].astype(F32)
        for b in range(1, ranks):
            hidden = hidden + arr_ref[source + b * exps].astype(F32)
        scale = lax.rsqrt(jnp.sum(hidden * hidden, axis=1, keepdims=True) * (1.0 / D) + 1e-06)
        normed_ref[k] = (hidden * scale * gain_ref[...]).astype(BF16)
    width = att_ref.shape[1]
    place = lax.axis_index("tok")
    mine = lax.axis_index("exp")

    def gather(slot):
        total = raw_ref[...]
        for b in range(ranks):
            part = arr_ref[mine + b * exps, :, slot].astype(F32)
            total = total + jnp.where(place == b, 0.0, part)
        att_ref[...] = total

    if width % LANES == 0:
        gather(pl.ds(pl.multiple_of(place * width, LANES), width))
    else:
        for b in range(ranks):
            pl.when(place == b)(functools.partial(gather, slice(b * width, (b + 1) * width)))


def expert_kernel(ids_ref, gates_ref, *refs, ranks, packed):
    subs, exps, rows, _ = ids_ref.shape
    sources = refs[:subs]
    wg_ref, wu_ref, wd_ref, out_ref, lhs = refs[subs:]
    for k in range(ranks):
        lhs[rows * k : rows * (k + 1), :] = sources[k % subs][k // subs].astype(F32)
    x = lhs[...].astype(BF16)
    gate = jnp.dot(x, wg_ref[0], preferred_element_type=F32)
    up = jnp.dot(x, wu_ref[0], preferred_element_type=F32)
    act = (gate / (1.0 + jnp.exp(-gate)) * up).astype(BF16)
    y = jnp.dot(act, wd_ref[0], preferred_element_type=F32)
    mine = lax.axis_index("tok") * subs + lax.axis_index("sub")
    for k in range(ranks):
        e = lax.axis_index("exp") ^ (k // subs)
        s = lax.axis_index("sub") ^ (k % subs)
        named = jnp.where(ids_ref[s, e] == mine, gates_ref[s, e], 0.0)
        lhs[rows * k : rows * (k + 1), :] = y[rows * k : rows * (k + 1), :] * jnp.sum(
            named, axis=1, keepdims=True
        )
    if not packed:
        out_ref[...] = lhs[...].astype(BF16)
        return
    half = ranks * rows // 2
    left = lax.broadcasted_iota(jnp.int32, (half, LANES), 1) < HALF
    for c in range(D // LANES):
        upper = lhs[:half, LANES * c : LANES * (c + 1)]
        lower = lhs[half:, LANES * c : LANES * (c + 1)]
        out_ref[2 * c] = jnp.where(left, upper, pltpu.roll(lower, HALF, 1)).astype(BF16)
        out_ref[2 * c + 1] = jnp.where(left, pltpu.roll(upper, HALF, 1), lower).astype(BF16)


def mix_kernel(arr_ref, att_ref, out_ref, final_ref):
    final_ref[...] = att_ref[...]
    subs, exps, rows, _ = out_ref.shape
    ranks = subs * exps
    half = ranks * rows // 2
    totals = []
    for g in range(ranks):
        total = arr_ref[g].astype(F32)
        for b in range(g + ranks, arr_ref.shape[0], ranks):
            total = total + arr_ref[b].astype(F32)
        totals.append(total)
    for j in range(ranks):
        mixed = None
        for g in range(ranks):
            row = (j ^ g) * rows
            lanes = slice(0, HALF) if row < half else slice(HALF, LANES)
            piece = totals[g][row % half : row % half + rows, lanes]
            mixed = piece if mixed is None else mixed + piece
        out_ref[j % subs, j // subs] = mixed


VMEM_SPEC = pl.BlockSpec(memory_space=pltpu.VMEM)
HBM_SPEC = pl.BlockSpec(memory_space=pltpu.HBM)


def call(kernel, shapes, in_specs, scratch, name, cost=0, limit=8 * 1024 * 1024):
    many = isinstance(shapes, (list, tuple))
    return pl.pallas_call(
        kernel,
        out_shape=shapes,
        in_specs=in_specs,
        out_specs=[VMEM_SPEC] * len(shapes) if many else VMEM_SPEC,
        scratch_shapes=scratch,
        name=name,
        cost_estimate=pl.CostEstimate(flops=cost, bytes_accessed=cost // 700, transcendentals=0),
        compiler_params=pltpu.CompilerParams(vmem_limit_bytes=limit),
    )


def body(
    query,
    key_cache_table,
    value_cache_table,
    latest_key,
    latest_value,
    lengths,
    resid,
    norm_gain,
    out_weight,
    expert_ids,
    gate_weights,
    w_gate,
    w_up,
    w_down,
):
    tok_ranks = lax.axis_size("tok")
    exp_ranks = lax.axis_size("exp")
    sub_ranks = lax.axis_size("sub")
    rows = query.shape[2]
    extent = key_cache_table.shape[3]
    feature_cols = resid.shape[3]
    own_heads = QUERY_HEADS // tok_ranks
    per = own_heads * rows
    keys = key_cache_table.reshape(rows, extent, KEY_VALUE_HEADS * HEAD_DIMENSION)
    values = value_cache_table.reshape(rows, extent, KEY_VALUE_HEADS * HEAD_DIMENSION)
    q = query.reshape(rows, QUERY_HEADS * HEAD_DIMENSION)
    shared_cols = KEY_VALUE_HEADS * HEAD_DIMENSION
    message, own = call(
        attend_kernel,
        [
            jax.ShapeDtypeStruct((QUERY_HEADS * rows, 2 * LANES), BF16),
            jax.ShapeDtypeStruct((per, 2 * LANES), F32),
        ],
        [HBM_SPEC] * 6,
        [
            pltpu.SMEM(lengths.shape, jnp.int32),
            pltpu.VMEM((rows, QUERY_HEADS * HEAD_DIMENSION), BF16),
            pltpu.VMEM((rows, shared_cols), BF16),
            pltpu.VMEM((rows, shared_cols), BF16),
            pltpu.VMEM((rows * extent, shared_cols), BF16),
            pltpu.VMEM((rows * extent, shared_cols), BF16),
            pltpu.VMEM((QUERY_HEADS * rows, HEAD_DIMENSION), F32),
            pltpu.SemaphoreType.DMA((3,)),
        ],
        "attend",
        cost=20_000_000_000,
    )(
        *(
            pltpu.with_memory_space_constraint(x, pltpu.HBM)
            for x in (
                lengths,
                q,
                latest_key.reshape(rows, shared_cols),
                latest_value.reshape(rows, shared_cols),
                keys,
                values,
            )
        )
    )
    arrived = lax.all_to_all(
        message.reshape(tok_ranks, per, 2 * LANES), "tok", split_axis=0, concat_axis=0, tiled=True
    )
    share, raw = call(
        project_kernel,
        [
            jax.ShapeDtypeStruct((tok_ranks * exp_ranks, rows, D), BF16),
            jax.ShapeDtypeStruct((rows, feature_cols), F32),
        ],
        [VMEM_SPEC] * 4,
        [pltpu.VMEM((per, LANES), F32), pltpu.VMEM((rows, D), F32)],
        "project",
        cost=20_000_000_000,
    )(arrived, own, resid.reshape(rows, feature_cols), out_weight)
    shares = lax.all_to_all(share, ("tok", "exp"), split_axis=0, concat_axis=0, tiled=True)
    attended, normed = call(
        norm_kernel,
        [
            jax.ShapeDtypeStruct((rows, feature_cols), F32),
            jax.ShapeDtypeStruct((exp_ranks, rows, D), BF16),
        ],
        [VMEM_SPEC] * 3,
        [],
        "norm",
    )(shares, raw, norm_gain.reshape(1, D))
    ranks = exp_ranks * sub_ranks
    pieces = [normed] + [
        lax.ppermute(normed, "sub", [(i, i ^ k) for i in range(sub_ranks)])
        for k in range(1, sub_ranks)
    ]
    block_cols = D // (tok_ranks * ranks)
    packed = 2 * block_cols == LANES
    rows_all = ranks * rows
    shape = (tok_ranks * ranks, rows_all // 2, LANES) if packed else (rows_all, D)
    weighted = call(
        functools.partial(expert_kernel, ranks=ranks, packed=packed),
        jax.ShapeDtypeStruct(shape, BF16),
        [VMEM_SPEC] * (5 + sub_ranks),
        [pltpu.VMEM((rows_all, D), F32)],
        "experts",
    )(expert_ids, gate_weights, *pieces, w_gate, w_up, w_down)
    everywhere = ("tok", "exp", "sub")
    if packed:
        received = lax.all_to_all(weighted, everywhere, split_axis=0, concat_axis=0, tiled=True)
        expert_mix, attended = call(
            mix_kernel,
            [
                jax.ShapeDtypeStruct((sub_ranks, exp_ranks, rows, block_cols), F32),
                jax.ShapeDtypeStruct((rows, feature_cols), F32),
            ],
            [VMEM_SPEC] * 2,
            [],
            "mix",
        )(received, attended)
    else:
        blocks = jnp.transpose(weighted.reshape(rows_all, tok_ranks * ranks, block_cols), (1, 0, 2))
        received = lax.all_to_all(blocks, everywhere, split_axis=0, concat_axis=0, tiled=True)
        grouped = jnp.sum(
            received.astype(F32).reshape(tok_ranks, ranks, ranks, rows, block_cols), axis=0
        )
        mixed = [sum(grouped[g, j ^ g] for g in range(ranks)) for j in range(ranks)]
        expert_mix = jnp.transpose(
            jnp.stack(mixed).reshape(exp_ranks, sub_ranks, rows, block_cols), (1, 0, 2, 3)
        )
    return (attended.reshape(1, 1, rows, feature_cols), expert_mix)


def solution(mesh):
    placed = (
        P(("groups", "sub"), "exp", None, None),
        P(("groups", "sub"), "exp", None, "tok", None),
        P(("groups", "sub"), "exp", None, "tok", None),
        P(("groups", "sub"), "exp", None, None),
        P(("groups", "sub"), "exp", None, None),
        P(("groups", "sub"), "exp", None),
        P(("groups", "sub"), "exp", None, "tok"),
        P(),
        P("tok", None),
        P("groups", None, None, None),
        P("groups", None, None, None),
        P(("tok", "sub"), None, "exp"),
        P(("tok", "sub"), None, "exp"),
        P(("tok", "sub"), "exp", None),
    )
    return jax.shard_map(
        body,
        mesh=mesh,
        in_specs=placed,
        out_specs=(
            P(("groups", "sub"), "exp", None, "tok"),
            P("groups", None, None, ("tok", "exp", "sub")),
        ),
        check_vma=False,
    )
```

```python
import functools

import jax
import jax.numpy as jnp
from jax import lax
from jax.experimental import pallas as pl
from jax.experimental.pallas import tpu as pltpu
from jax.sharding import PartitionSpec as P

D = 2048
QUERY_HEADS = 32
KEY_VALUE_HEADS = 4
HEAD_DIMENSION = 128
TOPK = 8
GROUP = QUERY_HEADS // KEY_VALUE_HEADS
SCALE = HEAD_DIMENSION ** (-0.5)
LANES = 128
HALF = 64
PIECES = 8

F32 = jnp.float32
BF16 = jnp.bfloat16


def attend_kernel(
    len_hbm,
    q_hbm,
    lk_hbm,
    lv_hbm,
    k_hbm,
    v_hbm,
    msg_ref,
    own_ref,
    len_ref,
    q_ref,
    lk_ref,
    lv_ref,
    kbuf,
    vbuf,
    qs,
    sems,
):
    rows = q_ref.shape[0]
    extent = k_hbm.shape[1]
    own_heads = own_ref.shape[0] // rows
    block = GROUP * rows
    cut = extent // PIECES
    copies = [
        pltpu.make_async_copy(source, target, sems.at[0])
        for source, target in (
            (q_hbm, q_ref),
            (len_hbm, len_ref),
            (lk_hbm, lk_ref),
            (lv_hbm, lv_ref),
        )
    ]
    early = len(copies)
    for which, (source, target) in enumerate(((k_hbm, kbuf), (v_hbm, vbuf))):
        for r in range(rows):
            for c in range(PIECES):
                copies.append(
                    pltpu.make_async_copy(
                        source.at[r, pl.ds(cut * c, cut)],
                        target.at[pl.ds(r * extent + cut * c, cut)],
                        sems.at[1 + which],
                    )
                )
    middle = early + rows * PIECES
    for n, copy in enumerate(copies):
        copy.start(priority=1 if n >= middle else 0)
    for copy in copies[:early]:
        copy.wait()
    place = lax.axis_index("tok")
    for h in range(QUERY_HEADS):
        qs[rows * h : rows * (h + 1), :] = q_ref[
            :, HEAD_DIMENSION * h : HEAD_DIMENSION * (h + 1)
        ].astype(F32)
    for j in range(own_heads):
        head = place * own_heads + j
        mine = pl.ds(pl.multiple_of(head * HEAD_DIMENSION, HEAD_DIMENSION), HEAD_DIMENSION)
        shared = pl.ds(
            pl.multiple_of((head // GROUP) * HEAD_DIMENSION, HEAD_DIMENSION), HEAD_DIMENSION
        )
        product = q_ref[:, mine].astype(F32) * lk_ref[:, shared].astype(F32)
        own_ref[rows * j : rows * (j + 1), LANES:] = jnp.broadcast_to(
            jnp.sum(product, axis=1, keepdims=True) * SCALE, (rows, LANES)
        )
        own_ref[rows * j : rows * (j + 1), :LANES] = lv_ref[:, shared].astype(F32)
    row_id = lax.rem(lax.broadcasted_iota(jnp.int32, (block, 1), 0), rows)
    limit = jnp.zeros((block, 1), jnp.int32)
    for r in range(rows):
        limit = jnp.where(row_id == r, len_ref[0, 0, r], limit)
    first = place * extent
    usable = first + lax.broadcasted_iota(jnp.int32, (block, extent), 1) < limit
    lane = lax.broadcasted_iota(jnp.int32, (block, LANES), 1)
    queries = [qs[block * h : block * (h + 1), :].astype(BF16) for h in range(KEY_VALUE_HEADS)]
    for copy in copies[early:]:
        copy.wait()
    wides, shares = [], []
    for h in range(KEY_VALUE_HEADS):
        part = slice(HEAD_DIMENSION * h, HEAD_DIMENSION * (h + 1))
        full = lax.dot_general(
            queries[h], kbuf[:, part], (((1,), (1,)), ((), ())), preferred_element_type=F32
        )
        score = full[:, :extent]
        for r in range(1, rows):
            score = jnp.where(row_id == r, full[:, extent * r : extent * (r + 1)], score)
        masked = jnp.where(usable, score * SCALE, -1e30)
        peak = jnp.max(masked, axis=1, keepdims=True).astype(BF16).astype(F32)
        weight = jnp.where(usable, jnp.exp(masked - peak), 0.0).astype(BF16).astype(F32)
        total = jnp.sum(weight, axis=1, keepdims=True)
        wides.append(
            jnp.concatenate(
                [jnp.where(row_id == r, weight, 0.0) for r in range(rows)], axis=1
            ).astype(BF16)
        )
        shares.append(1.0 / jnp.where(total > 0.0, total, 1.0))
        high = total.astype(BF16).astype(F32)
        extra = jnp.where(lane == 0, peak, jnp.where(lane == 1, high, total - high))
        msg_ref[block * h : block * (h + 1), LANES:] = extra.astype(BF16)
    for h in range(KEY_VALUE_HEADS):
        part = slice(HEAD_DIMENSION * h, HEAD_DIMENSION * (h + 1))
        value = jnp.dot(wides[h], vbuf[:, part], preferred_element_type=F32) * shares[h]
        msg_ref[block * h : block * (h + 1), :LANES] = value.astype(BF16)


def project_kernel(arr_ref, own_ref, mine_ref, w_ref, msg_ref, raw_ref, hs, held):
    ranks, per, _ = arr_ref.shape
    rows, width = mine_ref.shape
    own_heads = per // rows
    own_score = own_ref[:, LANES : LANES + 1]
    stats = [arr_ref[b, :, LANES:].astype(F32) for b in range(ranks)]
    top = own_score
    for b in range(ranks):
        top = jnp.maximum(top, stats[b][:, 0:1])
    self_weight = jnp.exp(own_score - top)
    combined = self_weight * own_ref[:, :LANES]
    below = self_weight
    for b in range(ranks):
        factor = (stats[b][:, 1:2] + stats[b][:, 2:3]) * jnp.exp(stats[b][:, 0:1] - top)
        combined = combined + factor * arr_ref[b, :, :LANES].astype(F32)
        below = below + factor
    hs[...] = combined / below
    heads = jnp.concatenate(
        [hs[rows * j : rows * (j + 1), :] for j in range(own_heads)], axis=1
    ).astype(BF16)
    out = jnp.dot(heads, w_ref[...], preferred_element_type=F32)
    held[...] = out
    place = lax.axis_index("tok")
    if width % LANES == 0:
        slot = pl.ds(pl.multiple_of(place * width, LANES), width)
        raw_ref[...] = held[:, slot]
        held[:, slot] = raw_ref[...] + mine_ref[...].astype(F32)
    else:
        for b in range(ranks):

            @pl.when(place == b)
            def _():
                slot = slice(b * width, (b + 1) * width)
                raw_ref[...] = held[:, slot]
                held[:, slot] = raw_ref[...] + mine_ref[...].astype(F32)

    sent = held[...].astype(BF16)
    for b in range(msg_ref.shape[0]):
        msg_ref[b] = sent


def norm_kernel(arr_ref, raw_ref, gain_ref, att_ref, normed_ref, held):
    rows = raw_ref.shape[0]
    exps = normed_ref.shape[0] // rows
    ranks = arr_ref.shape[0] // exps
    for k in range(exps):
        source = lax.axis_index("exp") ^ k
        hidden = arr_ref[source].astype(F32)
        for b in range(1, ranks):
            hidden = hidden + arr_ref[source + b * exps].astype(F32)
        scale = lax.rsqrt(jnp.sum(hidden * hidden, axis=1, keepdims=True) * (1.0 / D) + 1e-06)
        held[rows * k : rows * (k + 1), :] = hidden * scale * gain_ref[...]
    normed_ref[...] = held[...].astype(BF16)
    width = att_ref.shape[1]
    place = lax.axis_index("tok")
    mine = lax.axis_index("exp")

    def gather(slot):
        total = raw_ref[...]
        for b in range(ranks):
            part = arr_ref[mine + b * exps, :, slot].astype(F32)
            total = total + jnp.where(place == b, 0.0, part)
        att_ref[...] = total

    if width % LANES == 0:
        gather(pl.ds(pl.multiple_of(place * width, LANES), width))
    else:
        for b in range(ranks):
            pl.when(place == b)(functools.partial(gather, slice(b * width, (b + 1) * width)))


def expert_kernel(ids_ref, gates_ref, *refs, packed):
    subs, exps, rows, _ = ids_ref.shape
    sources = refs[:subs]
    wg_ref, wu_ref, wd_ref, out_ref, gains = refs[subs:]
    mine = lax.axis_index("tok") * subs + lax.axis_index("sub")
    for k in range(subs * exps):
        s = lax.axis_index("sub") ^ (k // exps)
        e = lax.axis_index("exp") ^ (k % exps)
        named = jnp.where(ids_ref[s, e] == mine, gates_ref[s, e], 0.0)
        gains[rows * k : rows * (k + 1), :] = jnp.broadcast_to(
            jnp.sum(named, axis=1, keepdims=True), (rows, LANES)
        )
    x = jnp.concatenate([ref[...].astype(F32) for ref in sources], axis=0).astype(BF16)
    gate = jnp.dot(x, wg_ref[0], preferred_element_type=F32)
    up = jnp.dot(x, wu_ref[0], preferred_element_type=F32)
    act = (gate / (1.0 + jnp.exp(-gate)) * up * gains[:, :1]).astype(BF16)
    y = jnp.dot(act, wd_ref[0], preferred_element_type=F32)
    if not packed:
        out_ref[...] = y.astype(BF16)
        return
    half = y.shape[0] // 2
    left = lax.broadcasted_iota(jnp.int32, (half, LANES), 1) < HALF
    for c in range(D // LANES):
        upper = y[:half, LANES * c : LANES * (c + 1)]
        lower = y[half:, LANES * c : LANES * (c + 1)]
        out_ref[2 * c] = jnp.where(left, upper, pltpu.roll(lower, HALF, 1)).astype(BF16)
        out_ref[2 * c + 1] = jnp.where(left, pltpu.roll(upper, HALF, 1), lower).astype(BF16)


def mix_kernel(arr_ref, att_ref, out_ref, final_ref):
    final_ref[...] = att_ref[...]
    subs, exps, rows, _ = out_ref.shape
    ranks = subs * exps
    half = ranks * rows // 2
    totals = []
    for g in range(ranks):
        total = arr_ref[g].astype(F32)
        for b in range(g + ranks, arr_ref.shape[0], ranks):
            total = total + arr_ref[b].astype(F32)
        totals.append(total)
    for j in range(ranks):
        mixed = None
        for g in range(ranks):
            k = j ^ g
            row = ((k % subs) * exps + k // subs) * rows
            lanes = slice(0, HALF) if row < half else slice(HALF, LANES)
            piece = totals[g][row % half : row % half + rows, lanes]
            mixed = piece if mixed is None else mixed + piece
        out_ref[j % subs, j // subs] = mixed


VMEM_SPEC = pl.BlockSpec(memory_space=pltpu.VMEM)
HBM_SPEC = pl.BlockSpec(memory_space=pltpu.HBM)


def call(kernel, shapes, in_specs, scratch, name, cost=0, limit=8 * 1024 * 1024):
    many = isinstance(shapes, (list, tuple))
    return pl.pallas_call(
        kernel,
        out_shape=shapes,
        in_specs=in_specs,
        out_specs=[VMEM_SPEC] * len(shapes) if many else VMEM_SPEC,
        scratch_shapes=scratch,
        name=name,
        cost_estimate=pl.CostEstimate(flops=cost, bytes_accessed=cost // 700, transcendentals=0),
        compiler_params=pltpu.CompilerParams(vmem_limit_bytes=limit),
    )


def body(
    query,
    key_cache_table,
    value_cache_table,
    latest_key,
    latest_value,
    lengths,
    resid,
    norm_gain,
    out_weight,
    expert_ids,
    gate_weights,
    w_gate,
    w_up,
    w_down,
):
    tok_ranks = lax.axis_size("tok")
    exp_ranks = lax.axis_size("exp")
    sub_ranks = lax.axis_size("sub")
    rows = query.shape[2]
    extent = key_cache_table.shape[3]
    feature_cols = resid.shape[3]
    own_heads = QUERY_HEADS // tok_ranks
    per = own_heads * rows
    keys = key_cache_table.reshape(rows, extent, KEY_VALUE_HEADS * HEAD_DIMENSION)
    values = value_cache_table.reshape(rows, extent, KEY_VALUE_HEADS * HEAD_DIMENSION)
    q = query.reshape(rows, QUERY_HEADS * HEAD_DIMENSION)
    shared_cols = KEY_VALUE_HEADS * HEAD_DIMENSION
    message, own = call(
        attend_kernel,
        [
            jax.ShapeDtypeStruct((QUERY_HEADS * rows, 2 * LANES), BF16),
            jax.ShapeDtypeStruct((per, 2 * LANES), F32),
        ],
        [HBM_SPEC] * 6,
        [
            pltpu.SMEM(lengths.shape, jnp.int32),
            pltpu.VMEM((rows, QUERY_HEADS * HEAD_DIMENSION), BF16),
            pltpu.VMEM((rows, shared_cols), BF16),
            pltpu.VMEM((rows, shared_cols), BF16),
            pltpu.VMEM((rows * extent, shared_cols), BF16),
            pltpu.VMEM((rows * extent, shared_cols), BF16),
            pltpu.VMEM((QUERY_HEADS * rows, HEAD_DIMENSION), F32),
            pltpu.SemaphoreType.DMA((3,)),
        ],
        "attend",
        cost=20_000_000_000,
    )(
        *(
            pltpu.with_memory_space_constraint(x, pltpu.HBM)
            for x in (
                lengths,
                q,
                latest_key.reshape(rows, shared_cols),
                latest_value.reshape(rows, shared_cols),
                keys,
                values,
            )
        )
    )
    arrived = lax.all_to_all(
        message.reshape(tok_ranks, per, 2 * LANES), "tok", split_axis=0, concat_axis=0, tiled=True
    )
    share, raw = call(
        project_kernel,
        [
            jax.ShapeDtypeStruct((tok_ranks * exp_ranks, rows, D), BF16),
            jax.ShapeDtypeStruct((rows, feature_cols), F32),
        ],
        [VMEM_SPEC] * 4,
        [pltpu.VMEM((per, LANES), F32), pltpu.VMEM((rows, D), F32)],
        "project",
        cost=20_000_000_000,
    )(arrived, own, resid.reshape(rows, feature_cols), out_weight)
    shares = lax.all_to_all(share, ("tok", "exp"), split_axis=0, concat_axis=0, tiled=True)
    attended, normed = call(
        norm_kernel,
        [
            jax.ShapeDtypeStruct((rows, feature_cols), F32),
            jax.ShapeDtypeStruct((exp_ranks * rows, D), BF16),
        ],
        [VMEM_SPEC] * 3,
        [pltpu.VMEM((exp_ranks * rows, D), F32)],
        "norm",
    )(shares, raw, norm_gain.reshape(1, D))
    ranks = exp_ranks * sub_ranks
    pieces = [normed] + [
        lax.ppermute(normed, "sub", [(i, i ^ k) for i in range(sub_ranks)])
        for k in range(1, sub_ranks)
    ]
    block_cols = D // (tok_ranks * ranks)
    packed = 2 * block_cols == LANES
    rows_all = ranks * rows
    shape = (tok_ranks * ranks, rows_all // 2, LANES) if packed else (rows_all, D)
    weighted = call(
        functools.partial(expert_kernel, packed=packed),
        jax.ShapeDtypeStruct(shape, BF16),
        [VMEM_SPEC] * (5 + sub_ranks),
        [pltpu.VMEM((rows_all, LANES), F32)],
        "experts",
    )(expert_ids, gate_weights, *pieces, w_gate, w_up, w_down)
    everywhere = ("tok", "exp", "sub")
    if packed:
        received = lax.all_to_all(weighted, everywhere, split_axis=0, concat_axis=0, tiled=True)
        expert_mix, attended = call(
            mix_kernel,
            [
                jax.ShapeDtypeStruct((sub_ranks, exp_ranks, rows, block_cols), F32),
                jax.ShapeDtypeStruct((rows, feature_cols), F32),
            ],
            [VMEM_SPEC] * 2,
            [],
            "mix",
        )(received, attended)
    else:
        blocks = jnp.transpose(weighted.reshape(rows_all, tok_ranks * ranks, block_cols), (1, 0, 2))
        received = lax.all_to_all(blocks, everywhere, split_axis=0, concat_axis=0, tiled=True)
        grouped = jnp.sum(
            received.astype(F32).reshape(tok_ranks, ranks, ranks, rows, block_cols), axis=0
        )
        order = [(k % sub_ranks) * exp_ranks + k // sub_ranks for k in range(ranks)]
        mixed = [sum(grouped[g, order[j ^ g]] for g in range(ranks)) for j in range(ranks)]
        expert_mix = jnp.transpose(
            jnp.stack(mixed).reshape(exp_ranks, sub_ranks, rows, block_cols), (1, 0, 2, 3)
        )
    return (attended.reshape(1, 1, rows, feature_cols), expert_mix)


def solution(mesh):
    placed = (
        P(("groups", "sub"), "exp", None, None),
        P(("groups", "sub"), "exp", None, "tok", None),
        P(("groups", "sub"), "exp", None, "tok", None),
        P(("groups", "sub"), "exp", None, None),
        P(("groups", "sub"), "exp", None, None),
        P(("groups", "sub"), "exp", None),
        P(("groups", "sub"), "exp", None, "tok"),
        P(),
        P("tok", None),
        P("groups", None, None, None),
        P("groups", None, None, None),
        P(("tok", "sub"), None, "exp"),
        P(("tok", "sub"), None, "exp"),
        P(("tok", "sub"), "exp", None),
    )
    return jax.shard_map(
        body,
        mesh=mesh,
        in_specs=placed,
        out_specs=(
            P(("groups", "sub"), "exp", None, "tok"),
            P("groups", None, None, ("tok", "exp", "sub")),
        ),
        check_vma=False,
    )
```

```python
import functools

import jax
import jax.numpy as jnp
from jax import lax
from jax.experimental import pallas as pl
from jax.experimental.pallas import tpu as pltpu
from jax.sharding import PartitionSpec as P

D = 2048
QUERY_HEADS = 32
KEY_VALUE_HEADS = 4
HEAD_DIMENSION = 128
TOPK = 8
GROUP = QUERY_HEADS // KEY_VALUE_HEADS
SCALE = HEAD_DIMENSION ** (-0.5)
LANES = 128
HALF = 64
PIECES = 8

F32 = jnp.float32
BF16 = jnp.bfloat16


def attend_kernel(
    len_hbm,
    q_hbm,
    lk_hbm,
    lv_hbm,
    k_hbm,
    v_hbm,
    msg_ref,
    own_ref,
    len_ref,
    q_ref,
    lk_ref,
    lv_ref,
    kbuf,
    vbuf,
    qs,
    sems,
):
    rows = q_ref.shape[0]
    extent = k_hbm.shape[1]
    own_heads = own_ref.shape[0] // rows
    block = GROUP * rows
    cut = extent // PIECES
    copies = [
        pltpu.make_async_copy(source, target, sems.at[0])
        for source, target in (
            (q_hbm, q_ref),
            (len_hbm, len_ref),
            (lk_hbm, lk_ref),
            (lv_hbm, lv_ref),
        )
    ]
    early = len(copies)
    for which, (source, target) in enumerate(((k_hbm, kbuf), (v_hbm, vbuf))):
        for r in range(rows):
            for c in range(PIECES):
                copies.append(
                    pltpu.make_async_copy(
                        source.at[r, pl.ds(cut * c, cut)],
                        target.at[pl.ds(r * extent + cut * c, cut)],
                        sems.at[1 + which],
                    )
                )
    middle = early + rows * PIECES
    for n, copy in enumerate(copies):
        copy.start(priority=1 if n >= middle else 0)
    for copy in copies[:early]:
        copy.wait()
    place = lax.axis_index("tok")
    for h in range(QUERY_HEADS):
        qs[rows * h : rows * (h + 1), :] = q_ref[
            :, HEAD_DIMENSION * h : HEAD_DIMENSION * (h + 1)
        ].astype(F32)
    for j in range(own_heads):
        head = place * own_heads + j
        mine = pl.ds(pl.multiple_of(head * HEAD_DIMENSION, HEAD_DIMENSION), HEAD_DIMENSION)
        shared = pl.ds(
            pl.multiple_of((head // GROUP) * HEAD_DIMENSION, HEAD_DIMENSION), HEAD_DIMENSION
        )
        product = q_ref[:, mine].astype(F32) * lk_ref[:, shared].astype(F32)
        own_ref[rows * j : rows * (j + 1), LANES:] = jnp.broadcast_to(
            jnp.sum(product, axis=1, keepdims=True) * SCALE, (rows, LANES)
        )
        own_ref[rows * j : rows * (j + 1), :LANES] = lv_ref[:, shared].astype(F32)
    row_id = lax.rem(lax.broadcasted_iota(jnp.int32, (block, 1), 0), rows)
    limit = jnp.zeros((block, 1), jnp.int32)
    for r in range(rows):
        limit = jnp.where(row_id == r, len_ref[0, 0, r], limit)
    first = place * extent
    usable = first + lax.broadcasted_iota(jnp.int32, (block, extent), 1) < limit
    queries = [qs[block * h : block * (h + 1), :].astype(BF16) for h in range(KEY_VALUE_HEADS)]
    for copy in copies[early:]:
        copy.wait()
    ranks, tall, across = msg_ref.shape
    groups = across // LANES - 1
    per = tall * groups
    lane = lax.broadcasted_iota(jnp.int32, (tall, LANES), 1)
    wides, shares = [], []
    for h in range(KEY_VALUE_HEADS):
        part = slice(HEAD_DIMENSION * h, HEAD_DIMENSION * (h + 1))
        full = lax.dot_general(
            queries[h], kbuf[:, part], (((1,), (1,)), ((), ())), preferred_element_type=F32
        )
        score = full[:, :extent]
        for r in range(1, rows):
            score = jnp.where(row_id == r, full[:, extent * r : extent * (r + 1)], score)
        masked = jnp.where(usable, score * SCALE, -1e30)
        peak = jnp.max(masked, axis=1, keepdims=True).astype(BF16).astype(F32)
        weight = jnp.where(usable, jnp.exp(masked - peak), 0.0).astype(BF16).astype(F32)
        total = jnp.sum(weight, axis=1, keepdims=True)
        wides.append(
            jnp.concatenate(
                [jnp.where(row_id == r, weight, 0.0) for r in range(rows)], axis=1
            ).astype(BF16)
        )
        shares.append(1.0 / jnp.where(total > 0.0, total, 1.0))
        high = total.astype(BF16).astype(F32)
        low = total - high
        for d in range(block // per):
            extra = jnp.zeros((tall, LANES), F32)
            for c in range(groups):
                some = slice(per * d + tall * c, per * d + tall * (c + 1))
                extra = jnp.where(lane == 3 * c, peak[some], extra)
                extra = jnp.where(lane == 3 * c + 1, high[some], extra)
                extra = jnp.where(lane == 3 * c + 2, low[some], extra)
            msg_ref[h * (block // per) + d, :, groups * LANES :] = extra.astype(BF16)
    for h in range(KEY_VALUE_HEADS):
        part = slice(HEAD_DIMENSION * h, HEAD_DIMENSION * (h + 1))
        value = jnp.dot(wides[h], vbuf[:, part], preferred_element_type=F32) * shares[h]
        for d in range(block // per):
            for c in range(groups):
                msg_ref[h * (block // per) + d, :, LANES * c : LANES * (c + 1)] = value[
                    per * d + tall * c : per * d + tall * (c + 1)
                ].astype(BF16)


def project_kernel(arr_ref, own_ref, mine_ref, w_ref, msg_ref, raw_ref, hs, held):
    ranks, tall, across = arr_ref.shape
    groups = across // LANES - 1
    rows, width = mine_ref.shape
    own_heads = tall * groups // rows
    lane = lax.broadcasted_iota(jnp.int32, (tall, LANES), 1)
    own_score = jnp.full((tall, LANES), -1e30, F32)
    for c in range(groups):
        own_score = jnp.where(
            lane == 3 * c, own_ref[tall * c : tall * (c + 1), LANES:], own_score
        )
    stats = [arr_ref[b, :, groups * LANES :].astype(F32) for b in range(ranks)]
    top = own_score
    for b in range(ranks):
        top = jnp.maximum(top, stats[b])
    self_weight = jnp.exp(own_score - top)
    below = self_weight
    factors = []
    for b in range(ranks):
        total = pltpu.roll(stats[b], LANES - 1, 1) + pltpu.roll(stats[b], LANES - 2, 1)
        factors.append(total * jnp.exp(stats[b] - top))
        below = below + factors[b]
    for c in range(groups):
        some = slice(tall * c, tall * (c + 1))
        column = slice(3 * c, 3 * c + 1)
        combined = self_weight[:, column] * own_ref[some, :LANES]
        for b in range(ranks):
            combined = combined + factors[b][:, column] * arr_ref[
                b, :, LANES * c : LANES * (c + 1)
            ].astype(F32)
        hs[some, :] = combined / below[:, column]
    heads = jnp.concatenate(
        [hs[rows * j : rows * (j + 1), :] for j in range(own_heads)], axis=1
    ).astype(BF16)
    out = jnp.dot(heads, w_ref[...], preferred_element_type=F32)
    held[...] = out
    place = lax.axis_index("tok")
    if width % LANES == 0:
        slot = pl.ds(pl.multiple_of(place * width, LANES), width)
        raw_ref[...] = held[:, slot]
        held[:, slot] = raw_ref[...] + mine_ref[...].astype(F32)
    else:
        for b in range(ranks):

            @pl.when(place == b)
            def _():
                slot = slice(b * width, (b + 1) * width)
                raw_ref[...] = held[:, slot]
                held[:, slot] = raw_ref[...] + mine_ref[...].astype(F32)

    sent = held[...].astype(BF16)
    for b in range(msg_ref.shape[0]):
        msg_ref[b] = sent


def norm_kernel(arr_ref, raw_ref, gain_ref, att_ref, normed_ref, held):
    rows = raw_ref.shape[0]
    exps = normed_ref.shape[0] // rows
    ranks = arr_ref.shape[0] // exps
    for k in range(exps):
        source = lax.axis_index("exp") ^ k
        hidden = arr_ref[source].astype(F32)
        for b in range(1, ranks):
            hidden = hidden + arr_ref[source + b * exps].astype(F32)
        scale = lax.rsqrt(jnp.sum(hidden * hidden, axis=1, keepdims=True) * (1.0 / D) + 1e-06)
        held[rows * k : rows * (k + 1), :] = hidden * scale * gain_ref[...]
    normed_ref[...] = held[...].astype(BF16)
    width = att_ref.shape[1]
    place = lax.axis_index("tok")
    mine = lax.axis_index("exp")

    def gather(slot):
        total = raw_ref[...]
        for b in range(ranks):
            part = arr_ref[mine + b * exps, :, slot].astype(F32)
            total = total + jnp.where(place == b, 0.0, part)
        att_ref[...] = total

    if width % LANES == 0:
        gather(pl.ds(pl.multiple_of(place * width, LANES), width))
    else:
        for b in range(ranks):
            pl.when(place == b)(functools.partial(gather, slice(b * width, (b + 1) * width)))


def expert_kernel(ids_ref, gates_ref, *refs, packed):
    subs, exps, rows, _ = ids_ref.shape
    sources = refs[:subs]
    wg_ref, wu_ref, wd_ref, out_ref, gains = refs[subs:]
    mine = lax.axis_index("tok") * subs + lax.axis_index("sub")
    for k in range(subs * exps):
        s = lax.axis_index("sub") ^ (k // exps)
        e = lax.axis_index("exp") ^ (k % exps)
        named = jnp.where(ids_ref[s, e] == mine, gates_ref[s, e], 0.0)
        gains[rows * k : rows * (k + 1), :] = jnp.broadcast_to(
            jnp.sum(named, axis=1, keepdims=True), (rows, LANES)
        )
    x = jnp.concatenate([ref[...].astype(F32) for ref in sources], axis=0).astype(BF16)
    gate = jnp.dot(x, wg_ref[0], preferred_element_type=F32)
    up = jnp.dot(x, wu_ref[0], preferred_element_type=F32)
    act = (gate / (1.0 + jnp.exp(-gate)) * up * gains[:, :1]).astype(BF16)
    y = jnp.dot(act, wd_ref[0], preferred_element_type=F32)
    if not packed:
        out_ref[...] = y.astype(BF16)
        return
    half = y.shape[0] // 2
    left = lax.broadcasted_iota(jnp.int32, (half, LANES), 1) < HALF
    for c in range(D // LANES):
        upper = y[:half, LANES * c : LANES * (c + 1)]
        lower = y[half:, LANES * c : LANES * (c + 1)]
        out_ref[2 * c] = jnp.where(left, upper, pltpu.roll(lower, HALF, 1)).astype(BF16)
        out_ref[2 * c + 1] = jnp.where(left, pltpu.roll(upper, HALF, 1), lower).astype(BF16)


def mix_kernel(arr_ref, att_ref, out_ref, final_ref):
    final_ref[...] = att_ref[...]
    subs, exps, rows, _ = out_ref.shape
    ranks = subs * exps
    half = ranks * rows // 2
    totals = []
    for g in range(ranks):
        total = arr_ref[g].astype(F32)
        for b in range(g + ranks, arr_ref.shape[0], ranks):
            total = total + arr_ref[b].astype(F32)
        totals.append(total)
    for j in range(ranks):
        mixed = None
        for g in range(ranks):
            k = j ^ g
            row = ((k % subs) * exps + k // subs) * rows
            lanes = slice(0, HALF) if row < half else slice(HALF, LANES)
            piece = totals[g][row % half : row % half + rows, lanes]
            mixed = piece if mixed is None else mixed + piece
        out_ref[j % subs, j // subs] = mixed


VMEM_SPEC = pl.BlockSpec(memory_space=pltpu.VMEM)
HBM_SPEC = pl.BlockSpec(memory_space=pltpu.HBM)


def call(kernel, shapes, in_specs, scratch, name, cost=0, limit=8 * 1024 * 1024):
    many = isinstance(shapes, (list, tuple))
    return pl.pallas_call(
        kernel,
        out_shape=shapes,
        in_specs=in_specs,
        out_specs=[VMEM_SPEC] * len(shapes) if many else VMEM_SPEC,
        scratch_shapes=scratch,
        name=name,
        cost_estimate=pl.CostEstimate(flops=cost, bytes_accessed=cost // 700, transcendentals=0),
        compiler_params=pltpu.CompilerParams(vmem_limit_bytes=limit),
    )


def body(
    query,
    key_cache_table,
    value_cache_table,
    latest_key,
    latest_value,
    lengths,
    resid,
    norm_gain,
    out_weight,
    expert_ids,
    gate_weights,
    w_gate,
    w_up,
    w_down,
):
    tok_ranks = lax.axis_size("tok")
    exp_ranks = lax.axis_size("exp")
    sub_ranks = lax.axis_size("sub")
    rows = query.shape[2]
    extent = key_cache_table.shape[3]
    feature_cols = resid.shape[3]
    own_heads = QUERY_HEADS // tok_ranks
    per = own_heads * rows
    groups = max(1, per // 8)
    keys = key_cache_table.reshape(rows, extent, KEY_VALUE_HEADS * HEAD_DIMENSION)
    values = value_cache_table.reshape(rows, extent, KEY_VALUE_HEADS * HEAD_DIMENSION)
    q = query.reshape(rows, QUERY_HEADS * HEAD_DIMENSION)
    shared_cols = KEY_VALUE_HEADS * HEAD_DIMENSION
    message, own = call(
        attend_kernel,
        [
            jax.ShapeDtypeStruct((tok_ranks, per // groups, (groups + 1) * LANES), BF16),
            jax.ShapeDtypeStruct((per, 2 * LANES), F32),
        ],
        [HBM_SPEC] * 6,
        [
            pltpu.SMEM(lengths.shape, jnp.int32),
            pltpu.VMEM((rows, QUERY_HEADS * HEAD_DIMENSION), BF16),
            pltpu.VMEM((rows, shared_cols), BF16),
            pltpu.VMEM((rows, shared_cols), BF16),
            pltpu.VMEM((rows * extent, shared_cols), BF16),
            pltpu.VMEM((rows * extent, shared_cols), BF16),
            pltpu.VMEM((QUERY_HEADS * rows, HEAD_DIMENSION), F32),
            pltpu.SemaphoreType.DMA((3,)),
        ],
        "attend",
        cost=20_000_000_000,
    )(
        *(
            pltpu.with_memory_space_constraint(x, pltpu.HBM)
            for x in (
                lengths,
                q,
                latest_key.reshape(rows, shared_cols),
                latest_value.reshape(rows, shared_cols),
                keys,
                values,
            )
        )
    )
    arrived = lax.all_to_all(message, "tok", split_axis=0, concat_axis=0, tiled=True)
    share, raw = call(
        project_kernel,
        [
            jax.ShapeDtypeStruct((tok_ranks * exp_ranks, rows, D), BF16),
            jax.ShapeDtypeStruct((rows, feature_cols), F32),
        ],
        [VMEM_SPEC] * 4,
        [pltpu.VMEM((per, LANES), F32), pltpu.VMEM((rows, D), F32)],
        "project",
        cost=20_000_000_000,
    )(arrived, own, resid.reshape(rows, feature_cols), out_weight)
    shares = lax.all_to_all(share, ("tok", "exp"), split_axis=0, concat_axis=0, tiled=True)
    attended, normed = call(
        norm_kernel,
        [
            jax.ShapeDtypeStruct((rows, feature_cols), F32),
            jax.ShapeDtypeStruct((exp_ranks * rows, D), BF16),
        ],
        [VMEM_SPEC] * 3,
        [pltpu.VMEM((exp_ranks * rows, D), F32)],
        "norm",
    )(shares, raw, norm_gain.reshape(1, D))
    ranks = exp_ranks * sub_ranks
    pieces = [normed] + [
        lax.ppermute(normed, "sub", [(i, i ^ k) for i in range(sub_ranks)])
        for k in range(1, sub_ranks)
    ]
    block_cols = D // (tok_ranks * ranks)
    packed = 2 * block_cols == LANES
    rows_all = ranks * rows
    shape = (tok_ranks * ranks, rows_all // 2, LANES) if packed else (rows_all, D)
    weighted = call(
        functools.partial(expert_kernel, packed=packed),
        jax.ShapeDtypeStruct(shape, BF16),
        [VMEM_SPEC] * (5 + sub_ranks),
        [pltpu.VMEM((rows_all, LANES), F32)],
        "experts",
    )(expert_ids, gate_weights, *pieces, w_gate, w_up, w_down)
    everywhere = ("tok", "exp", "sub")
    if packed:
        received = lax.all_to_all(weighted, everywhere, split_axis=0, concat_axis=0, tiled=True)
        expert_mix, attended = call(
            mix_kernel,
            [
                jax.ShapeDtypeStruct((sub_ranks, exp_ranks, rows, block_cols), F32),
                jax.ShapeDtypeStruct((rows, feature_cols), F32),
            ],
            [VMEM_SPEC] * 2,
            [],
            "mix",
        )(received, attended)
    else:
        blocks = jnp.transpose(weighted.reshape(rows_all, tok_ranks * ranks, block_cols), (1, 0, 2))
        received = lax.all_to_all(blocks, everywhere, split_axis=0, concat_axis=0, tiled=True)
        grouped = jnp.sum(
            received.astype(F32).reshape(tok_ranks, ranks, ranks, rows, block_cols), axis=0
        )
        order = [(k % sub_ranks) * exp_ranks + k // sub_ranks for k in range(ranks)]
        mixed = [sum(grouped[g, order[j ^ g]] for g in range(ranks)) for j in range(ranks)]
        expert_mix = jnp.transpose(
            jnp.stack(mixed).reshape(exp_ranks, sub_ranks, rows, block_cols), (1, 0, 2, 3)
        )
    return (attended.reshape(1, 1, rows, feature_cols), expert_mix)


def solution(mesh):
    placed = (
        P(("groups", "sub"), "exp", None, None),
        P(("groups", "sub"), "exp", None, "tok", None),
        P(("groups", "sub"), "exp", None, "tok", None),
        P(("groups", "sub"), "exp", None, None),
        P(("groups", "sub"), "exp", None, None),
        P(("groups", "sub"), "exp", None),
        P(("groups", "sub"), "exp", None, "tok"),
        P(),
        P("tok", None),
        P("groups", None, None, None),
        P("groups", None, None, None),
        P(("tok", "sub"), None, "exp"),
        P(("tok", "sub"), None, "exp"),
        P(("tok", "sub"), "exp", None),
    )
    return jax.shard_map(
        body,
        mesh=mesh,
        in_specs=placed,
        out_specs=(
            P(("groups", "sub"), "exp", None, "tok"),
            P("groups", None, None, ("tok", "exp", "sub")),
        ),
        check_vma=False,
    )
```

```python
import functools

import jax
import jax.numpy as jnp
from jax import lax
from jax.experimental import pallas as pl
from jax.experimental.pallas import tpu as pltpu
from jax.sharding import PartitionSpec as P

D = 2048
QUERY_HEADS = 32
KEY_VALUE_HEADS = 4
HEAD_DIMENSION = 128
TOPK = 8
GROUP = QUERY_HEADS // KEY_VALUE_HEADS
CUTS = 2
SCALE = HEAD_DIMENSION ** (-0.5)
LANES = 128
HALF = 64
PIECES = 16

F32 = jnp.float32
BF16 = jnp.bfloat16


def attend_kernel(
    len_hbm,
    q_hbm,
    lk_hbm,
    lv_hbm,
    k_hbm,
    v_hbm,
    msg_ref,
    own_ref,
    len_ref,
    q_ref,
    lk_ref,
    lv_ref,
    kbuf,
    vbuf,
    qs,
    sems,
):
    rows = q_ref.shape[0]
    extent = k_hbm.shape[1]
    own_heads = own_ref.shape[0] // rows
    block = GROUP * rows
    cut = extent // PIECES
    copies = [
        pltpu.make_async_copy(source, target, sems.at[0])
        for source, target in (
            (q_hbm, q_ref),
            (len_hbm, len_ref),
            (lk_hbm, lk_ref),
            (lv_hbm, lv_ref),
        )
    ]
    early = len(copies)
    for which, (source, target) in enumerate(((k_hbm, kbuf), (v_hbm, vbuf))):
        for r in range(rows):
            for c in range(PIECES):
                copies.append(
                    pltpu.make_async_copy(
                        source.at[r, pl.ds(cut * c, cut)],
                        target.at[pl.ds(r * extent + cut * c, cut)],
                        sems.at[1 + which],
                    )
                )
    middle = early + rows * PIECES
    for n, copy in enumerate(copies):
        copy.start(priority=1 if n >= middle else 0)
    for copy in copies[:early]:
        copy.wait()
    place = lax.axis_index("tok")
    for h in range(QUERY_HEADS):
        qs[rows * h : rows * (h + 1), :] = q_ref[
            :, HEAD_DIMENSION * h : HEAD_DIMENSION * (h + 1)
        ].astype(F32)
    for j in range(own_heads):
        head = place * own_heads + j
        mine = pl.ds(pl.multiple_of(head * HEAD_DIMENSION, HEAD_DIMENSION), HEAD_DIMENSION)
        shared = pl.ds(
            pl.multiple_of((head // GROUP) * HEAD_DIMENSION, HEAD_DIMENSION), HEAD_DIMENSION
        )
        product = q_ref[:, mine].astype(F32) * lk_ref[:, shared].astype(F32)
        own_ref[rows * j : rows * (j + 1), LANES:] = jnp.broadcast_to(
            jnp.sum(product, axis=1, keepdims=True) * SCALE, (rows, LANES)
        )
        own_ref[rows * j : rows * (j + 1), :LANES] = lv_ref[:, shared].astype(F32)
    row_id = lax.rem(lax.broadcasted_iota(jnp.int32, (block, 1), 0), rows)
    limit = jnp.zeros((block, 1), jnp.int32)
    for r in range(rows):
        limit = jnp.where(row_id == r, len_ref[0, 0, r], limit)
    first = place * extent
    usable = first + lax.broadcasted_iota(jnp.int32, (block, extent), 1) < limit
    queries = [qs[block * h : block * (h + 1), :].astype(BF16) for h in range(KEY_VALUE_HEADS)]
    for copy in copies[early:]:
        copy.wait()
    ranks, tall, across = msg_ref.shape
    groups = across // LANES - 1
    per = tall * groups
    lane = lax.broadcasted_iota(jnp.int32, (tall, LANES), 1)
    wides, shares = [], []
    for h in range(KEY_VALUE_HEADS):
        part = slice(HEAD_DIMENSION * h, HEAD_DIMENSION * (h + 1))
        full = lax.dot_general(
            queries[h], kbuf[:, part], (((1,), (1,)), ((), ())), preferred_element_type=F32
        )
        score = full[:, :extent]
        for r in range(1, rows):
            score = jnp.where(row_id == r, full[:, extent * r : extent * (r + 1)], score)
        masked = jnp.where(usable, score * SCALE, -1e30)
        peak = jnp.max(masked, axis=1, keepdims=True).astype(BF16).astype(F32)
        weight = jnp.where(usable, jnp.exp(masked - peak), 0.0).astype(BF16).astype(F32)
        total = jnp.sum(weight, axis=1, keepdims=True)
        wides.append(
            jnp.concatenate(
                [jnp.where(row_id == r, weight, 0.0) for r in range(rows)], axis=1
            ).astype(BF16)
        )
        shares.append(1.0 / jnp.where(total > 0.0, total, 1.0))
        high = total.astype(BF16).astype(F32)
        low = total - high
        for d in range(block // per):
            extra = jnp.zeros((tall, LANES), F32)
            for c in range(groups):
                some = slice(per * d + tall * c, per * d + tall * (c + 1))
                extra = jnp.where(lane == 3 * c, peak[some], extra)
                extra = jnp.where(lane == 3 * c + 1, high[some], extra)
                extra = jnp.where(lane == 3 * c + 2, low[some], extra)
            msg_ref[h * (block // per) + d, :, groups * LANES :] = extra.astype(BF16)
    for h in range(KEY_VALUE_HEADS):
        part = slice(HEAD_DIMENSION * h, HEAD_DIMENSION * (h + 1))
        value = jnp.dot(wides[h], vbuf[:, part], preferred_element_type=F32) * shares[h]
        for d in range(block // per):
            for c in range(groups):
                msg_ref[h * (block // per) + d, :, LANES * c : LANES * (c + 1)] = value[
                    per * d + tall * c : per * d + tall * (c + 1)
                ].astype(BF16)


def project_kernel(arr_ref, own_ref, mine_ref, w_ref, msg_ref, raw_ref, hs, held, placed):
    ranks, tall, across = arr_ref.shape
    groups = across // LANES - 1
    rows, width = mine_ref.shape
    own_heads = tall * groups // rows
    place = lax.axis_index("tok")
    placed[...] = jnp.zeros_like(placed)
    if width % LANES == 0:
        slot = pl.ds(pl.multiple_of(place * width, LANES), width)
        placed[:, slot] = mine_ref[...].astype(F32)
    else:
        for b in range(ranks):

            @pl.when(place == b)
            def _():
                placed[:, b * width : (b + 1) * width] = mine_ref[...].astype(F32)

    lane = lax.broadcasted_iota(jnp.int32, (tall, LANES), 1)
    own_score = jnp.full((tall, LANES), -1e30, F32)
    for c in range(groups):
        own_score = jnp.where(
            lane == 3 * c, own_ref[tall * c : tall * (c + 1), LANES:], own_score
        )
    stats = [arr_ref[b, :, groups * LANES :].astype(F32) for b in range(ranks)]
    top = own_score
    for b in range(ranks):
        top = jnp.maximum(top, stats[b])
    self_weight = jnp.exp(own_score - top)
    below = self_weight
    factors = []
    for b in range(ranks):
        total = pltpu.roll(stats[b], LANES - 1, 1) + pltpu.roll(stats[b], LANES - 2, 1)
        factors.append(total * jnp.exp(stats[b] - top))
        below = below + factors[b]
    for c in range(groups):
        some = slice(tall * c, tall * (c + 1))
        column = slice(3 * c, 3 * c + 1)
        combined = self_weight[:, column] * own_ref[some, :LANES]
        for b in range(ranks):
            combined = combined + factors[b][:, column] * arr_ref[
                b, :, LANES * c : LANES * (c + 1)
            ].astype(F32)
        hs[some, :] = combined / below[:, column]
    heads = jnp.concatenate(
        [hs[rows * j : rows * (j + 1), :] for j in range(own_heads)], axis=1
    ).astype(BF16)
    wide = D // CUTS
    for n in range(CUTS):
        some = slice(wide * n, wide * (n + 1))
        out = jnp.dot(heads, w_ref[:, some], preferred_element_type=F32)
        held[:, some] = out
        sent = (out + placed[:, some]).astype(BF16)
        for b in range(msg_ref.shape[0]):
            msg_ref[b, :, some] = sent
    if width % LANES == 0:
        raw_ref[...] = held[:, slot]
    else:
        for b in range(ranks):

            @pl.when(place == b)
            def _():
                raw_ref[...] = held[:, b * width : (b + 1) * width]


def norm_kernel(arr_ref, raw_ref, gain_ref, att_ref, normed_ref, held):
    rows = raw_ref.shape[0]
    exps = normed_ref.shape[0] // rows
    ranks = arr_ref.shape[0] // exps
    for k in range(exps):
        source = lax.axis_index("exp") ^ k
        hidden = arr_ref[source].astype(F32)
        for b in range(1, ranks):
            hidden = hidden + arr_ref[source + b * exps].astype(F32)
        scale = lax.rsqrt(jnp.sum(hidden * hidden, axis=1, keepdims=True) * (1.0 / D) + 1e-06)
        held[rows * k : rows * (k + 1), :] = hidden * scale * gain_ref[...]
    normed_ref[...] = held[...].astype(BF16)
    width = att_ref.shape[1]
    place = lax.axis_index("tok")
    mine = lax.axis_index("exp")

    def gather(slot):
        total = raw_ref[...]
        for b in range(ranks):
            part = arr_ref[mine + b * exps, :, slot].astype(F32)
            total = total + jnp.where(place == b, 0.0, part)
        att_ref[...] = total

    if width % LANES == 0:
        gather(pl.ds(pl.multiple_of(place * width, LANES), width))
    else:
        for b in range(ranks):
            pl.when(place == b)(functools.partial(gather, slice(b * width, (b + 1) * width)))


def expert_kernel(ids_ref, gates_ref, *refs, packed):
    subs, exps, rows, _ = ids_ref.shape
    sources = refs[:subs]
    wg_ref, wu_ref, wd_ref, out_ref, gains = refs[subs:]
    mine = lax.axis_index("tok") * subs + lax.axis_index("sub")
    for k in range(subs * exps):
        s = lax.axis_index("sub") ^ (k // exps)
        e = lax.axis_index("exp") ^ (k % exps)
        named = jnp.where(ids_ref[s, e] == mine, gates_ref[s, e], 0.0)
        gains[rows * k : rows * (k + 1), :] = jnp.broadcast_to(
            jnp.sum(named, axis=1, keepdims=True), (rows, LANES)
        )
    x = jnp.concatenate([ref[...].astype(F32) for ref in sources], axis=0).astype(BF16)
    gate = jnp.dot(x, wg_ref[0], preferred_element_type=F32)
    up = jnp.dot(x, wu_ref[0], preferred_element_type=F32)
    act = (gate / (1.0 + jnp.exp(-gate)) * up * gains[:, :1]).astype(BF16)
    if not packed:
        out_ref[...] = jnp.dot(act, wd_ref[0], preferred_element_type=F32).astype(BF16)
        return
    half = x.shape[0] // 2
    left = lax.broadcasted_iota(jnp.int32, (half, LANES), 1) < HALF
    wide = D // CUTS
    for n in range(CUTS):
        y = jnp.dot(act, wd_ref[0, :, wide * n : wide * (n + 1)], preferred_element_type=F32)
        for c in range(wide // LANES):
            upper = y[:half, LANES * c : LANES * (c + 1)]
            lower = y[half:, LANES * c : LANES * (c + 1)]
            place = 2 * (wide // LANES * n + c)
            out_ref[place] = jnp.where(left, upper, pltpu.roll(lower, HALF, 1)).astype(BF16)
            out_ref[place + 1] = jnp.where(left, pltpu.roll(upper, HALF, 1), lower).astype(BF16)


def mix_kernel(arr_ref, att_ref, out_ref, final_ref):
    final_ref[...] = att_ref[...]
    subs, exps, rows, _ = out_ref.shape
    ranks = subs * exps
    half = ranks * rows // 2
    totals = []
    for g in range(ranks):
        total = arr_ref[g].astype(F32)
        for b in range(g + ranks, arr_ref.shape[0], ranks):
            total = total + arr_ref[b].astype(F32)
        totals.append(total)
    for j in range(ranks):
        mixed = None
        for g in range(ranks):
            k = j ^ g
            row = ((k % subs) * exps + k // subs) * rows
            lanes = slice(0, HALF) if row < half else slice(HALF, LANES)
            piece = totals[g][row % half : row % half + rows, lanes]
            mixed = piece if mixed is None else mixed + piece
        out_ref[j % subs, j // subs] = mixed


VMEM_SPEC = pl.BlockSpec(memory_space=pltpu.VMEM)
HBM_SPEC = pl.BlockSpec(memory_space=pltpu.HBM)


def call(kernel, shapes, in_specs, scratch, name, cost=0, limit=8 * 1024 * 1024):
    many = isinstance(shapes, (list, tuple))
    return pl.pallas_call(
        kernel,
        out_shape=shapes,
        in_specs=in_specs,
        out_specs=[VMEM_SPEC] * len(shapes) if many else VMEM_SPEC,
        scratch_shapes=scratch,
        name=name,
        cost_estimate=pl.CostEstimate(flops=cost, bytes_accessed=cost // 700, transcendentals=0),
        compiler_params=pltpu.CompilerParams(vmem_limit_bytes=limit),
    )


def body(
    query,
    key_cache_table,
    value_cache_table,
    latest_key,
    latest_value,
    lengths,
    resid,
    norm_gain,
    out_weight,
    expert_ids,
    gate_weights,
    w_gate,
    w_up,
    w_down,
):
    tok_ranks = lax.axis_size("tok")
    exp_ranks = lax.axis_size("exp")
    sub_ranks = lax.axis_size("sub")
    rows = query.shape[2]
    extent = key_cache_table.shape[3]
    feature_cols = resid.shape[3]
    own_heads = QUERY_HEADS // tok_ranks
    per = own_heads * rows
    groups = max(1, per // 8)
    keys = key_cache_table.reshape(rows, extent, KEY_VALUE_HEADS * HEAD_DIMENSION)
    values = value_cache_table.reshape(rows, extent, KEY_VALUE_HEADS * HEAD_DIMENSION)
    q = query.reshape(rows, QUERY_HEADS * HEAD_DIMENSION)
    shared_cols = KEY_VALUE_HEADS * HEAD_DIMENSION
    message, own = call(
        attend_kernel,
        [
            jax.ShapeDtypeStruct((tok_ranks, per // groups, (groups + 1) * LANES), BF16),
            jax.ShapeDtypeStruct((per, 2 * LANES), F32),
        ],
        [HBM_SPEC] * 6,
        [
            pltpu.SMEM(lengths.shape, jnp.int32),
            pltpu.VMEM((rows, QUERY_HEADS * HEAD_DIMENSION), BF16),
            pltpu.VMEM((rows, shared_cols), BF16),
            pltpu.VMEM((rows, shared_cols), BF16),
            pltpu.VMEM((rows * extent, shared_cols), BF16),
            pltpu.VMEM((rows * extent, shared_cols), BF16),
            pltpu.VMEM((QUERY_HEADS * rows, HEAD_DIMENSION), F32),
            pltpu.SemaphoreType.DMA((3,)),
        ],
        "attend",
        cost=20_000_000_000,
    )(
        *(
            pltpu.with_memory_space_constraint(x, pltpu.HBM)
            for x in (
                lengths,
                q,
                latest_key.reshape(rows, shared_cols),
                latest_value.reshape(rows, shared_cols),
                keys,
                values,
            )
        )
    )
    arrived = lax.all_to_all(message, "tok", split_axis=0, concat_axis=0, tiled=True)
    share, raw = call(
        project_kernel,
        [
            jax.ShapeDtypeStruct((tok_ranks * exp_ranks, rows, D), BF16),
            jax.ShapeDtypeStruct((rows, feature_cols), F32),
        ],
        [VMEM_SPEC] * 4,
        [
            pltpu.VMEM((per, LANES), F32),
            pltpu.VMEM((rows, D), F32),
            pltpu.VMEM((rows, D), F32),
        ],
        "project",
        cost=20_000_000_000,
    )(arrived, own, resid.reshape(rows, feature_cols), out_weight)
    shares = lax.all_to_all(share, ("tok", "exp"), split_axis=0, concat_axis=0, tiled=True)
    attended, normed = call(
        norm_kernel,
        [
            jax.ShapeDtypeStruct((rows, feature_cols), F32),
            jax.ShapeDtypeStruct((exp_ranks * rows, D), BF16),
        ],
        [VMEM_SPEC] * 3,
        [pltpu.VMEM((exp_ranks * rows, D), F32)],
        "norm",
    )(shares, raw, norm_gain.reshape(1, D))
    ranks = exp_ranks * sub_ranks
    pieces = [normed] + [
        lax.ppermute(normed, "sub", [(i, i ^ k) for i in range(sub_ranks)])
        for k in range(1, sub_ranks)
    ]
    block_cols = D // (tok_ranks * ranks)
    packed = 2 * block_cols == LANES
    rows_all = ranks * rows
    shape = (tok_ranks * ranks, rows_all // 2, LANES) if packed else (rows_all, D)
    weighted = call(
        functools.partial(expert_kernel, packed=packed),
        jax.ShapeDtypeStruct(shape, BF16),
        [VMEM_SPEC] * (5 + sub_ranks),
        [pltpu.VMEM((rows_all, LANES), F32)],
        "experts",
    )(expert_ids, gate_weights, *pieces, w_gate, w_up, w_down)
    everywhere = ("tok", "exp", "sub")
    if packed:
        received = lax.all_to_all(weighted, everywhere, split_axis=0, concat_axis=0, tiled=True)
        expert_mix, attended = call(
            mix_kernel,
            [
                jax.ShapeDtypeStruct((sub_ranks, exp_ranks, rows, block_cols), F32),
                jax.ShapeDtypeStruct((rows, feature_cols), F32),
            ],
            [VMEM_SPEC] * 2,
            [],
            "mix",
        )(received, attended)
    else:
        blocks = jnp.transpose(weighted.reshape(rows_all, tok_ranks * ranks, block_cols), (1, 0, 2))
        received = lax.all_to_all(blocks, everywhere, split_axis=0, concat_axis=0, tiled=True)
        grouped = jnp.sum(
            received.astype(F32).reshape(tok_ranks, ranks, ranks, rows, block_cols), axis=0
        )
        order = [(k % sub_ranks) * exp_ranks + k // sub_ranks for k in range(ranks)]
        mixed = [sum(grouped[g, order[j ^ g]] for g in range(ranks)) for j in range(ranks)]
        expert_mix = jnp.transpose(
            jnp.stack(mixed).reshape(exp_ranks, sub_ranks, rows, block_cols), (1, 0, 2, 3)
        )
    return (attended.reshape(1, 1, rows, feature_cols), expert_mix)


def solution(mesh):
    placed = (
        P(("groups", "sub"), "exp", None, None),
        P(("groups", "sub"), "exp", None, "tok", None),
        P(("groups", "sub"), "exp", None, "tok", None),
        P(("groups", "sub"), "exp", None, None),
        P(("groups", "sub"), "exp", None, None),
        P(("groups", "sub"), "exp", None),
        P(("groups", "sub"), "exp", None, "tok"),
        P(),
        P("tok", None),
        P("groups", None, None, None),
        P("groups", None, None, None),
        P(("tok", "sub"), None, "exp"),
        P(("tok", "sub"), None, "exp"),
        P(("tok", "sub"), "exp", None),
    )
    return jax.shard_map(
        body,
        mesh=mesh,
        in_specs=placed,
        out_specs=(
            P(("groups", "sub"), "exp", None, "tok"),
            P("groups", None, None, ("tok", "exp", "sub")),
        ),
        check_vma=False,
    )
```

```python
import functools

import jax
import jax.numpy as jnp
from jax import lax
from jax.experimental import pallas as pl
from jax.experimental.pallas import tpu as pltpu
from jax.sharding import PartitionSpec as P

D = 2048
QUERY_HEADS = 32
KEY_VALUE_HEADS = 4
HEAD_DIMENSION = 128
TOPK = 8
GROUP = QUERY_HEADS // KEY_VALUE_HEADS
CUTS = 2
SCALE = HEAD_DIMENSION ** (-0.5)
LANES = 128
HALF = 64
PIECES = 16

F32 = jnp.float32
BF16 = jnp.bfloat16


def attend_kernel(
    len_hbm,
    q_hbm,
    lk_hbm,
    lv_hbm,
    k_hbm,
    v_hbm,
    msg_ref,
    own_ref,
    len_ref,
    q_ref,
    lk_ref,
    lv_ref,
    kbuf,
    vbuf,
    qs,
    sems,
):
    rows = q_ref.shape[0]
    extent = k_hbm.shape[1]
    own_heads = own_ref.shape[0] // rows
    block = GROUP * rows
    cut = extent // PIECES
    copies = [
        pltpu.make_async_copy(source, target, sems.at[0])
        for source, target in (
            (q_hbm, q_ref),
            (len_hbm, len_ref),
            (lk_hbm, lk_ref),
            (lv_hbm, lv_ref),
        )
    ]
    early = len(copies)
    for which, (source, target) in enumerate(((k_hbm, kbuf), (v_hbm, vbuf))):
        for r in range(rows):
            for c in range(PIECES):
                copies.append(
                    pltpu.make_async_copy(
                        source.at[r, pl.ds(cut * c, cut)],
                        target.at[pl.ds(r * extent + cut * c, cut)],
                        sems.at[1 + which],
                    )
                )
    middle = early + rows * PIECES
    for n, copy in enumerate(copies):
        copy.start(priority=1 if n >= middle else 0)
    for copy in copies[:early]:
        copy.wait()
    place = lax.axis_index("tok")
    for h in range(QUERY_HEADS):
        qs[rows * h : rows * (h + 1), :] = q_ref[
            :, HEAD_DIMENSION * h : HEAD_DIMENSION * (h + 1)
        ].astype(F32)
    for j in range(own_heads):
        head = place * own_heads + j
        mine = pl.ds(pl.multiple_of(head * HEAD_DIMENSION, HEAD_DIMENSION), HEAD_DIMENSION)
        shared = pl.ds(
            pl.multiple_of((head // GROUP) * HEAD_DIMENSION, HEAD_DIMENSION), HEAD_DIMENSION
        )
        product = q_ref[:, mine].astype(F32) * lk_ref[:, shared].astype(F32)
        own_ref[rows * j : rows * (j + 1), LANES:] = jnp.broadcast_to(
            jnp.sum(product, axis=1, keepdims=True) * SCALE, (rows, LANES)
        )
        own_ref[rows * j : rows * (j + 1), :LANES] = lv_ref[:, shared].astype(F32)
    row_id = lax.rem(lax.broadcasted_iota(jnp.int32, (block, 1), 0), rows)
    limit = jnp.zeros((block, 1), jnp.int32)
    for r in range(rows):
        limit = jnp.where(row_id == r, len_ref[0, 0, r], limit)
    first = place * extent
    usable = first + lax.broadcasted_iota(jnp.int32, (block, extent), 1) < limit
    queries = [qs[block * h : block * (h + 1), :].astype(BF16) for h in range(KEY_VALUE_HEADS)]
    for copy in copies[early:middle]:
        copy.wait()
    ranks, tall, across = msg_ref.shape
    groups = across // LANES - 1
    per = tall * groups
    lane = lax.broadcasted_iota(jnp.int32, (tall, LANES), 1)
    wides, shares = [], []
    for h in range(KEY_VALUE_HEADS):
        part = slice(HEAD_DIMENSION * h, HEAD_DIMENSION * (h + 1))
        full = lax.dot_general(
            queries[h], kbuf[:, part], (((1,), (1,)), ((), ())), preferred_element_type=F32
        )
        score = full[:, :extent]
        for r in range(1, rows):
            score = jnp.where(row_id == r, full[:, extent * r : extent * (r + 1)], score)
        masked = jnp.where(usable, score * SCALE, -1e30)
        peak = jnp.max(masked, axis=1, keepdims=True).astype(BF16).astype(F32)
        weight = jnp.where(usable, jnp.exp(masked - peak), 0.0).astype(BF16).astype(F32)
        total = jnp.sum(weight, axis=1, keepdims=True)
        wides.append(
            jnp.concatenate(
                [jnp.where(row_id == r, weight, 0.0) for r in range(rows)], axis=1
            ).astype(BF16)
        )
        shares.append(1.0 / jnp.where(total > 0.0, total, 1.0))
        high = total.astype(BF16).astype(F32)
        low = total - high
        for d in range(block // per):
            extra = jnp.zeros((tall, LANES), F32)
            for c in range(groups):
                some = slice(per * d + tall * c, per * d + tall * (c + 1))
                extra = jnp.where(lane == 3 * c, peak[some], extra)
                extra = jnp.where(lane == 3 * c + 1, high[some], extra)
                extra = jnp.where(lane == 3 * c + 2, low[some], extra)
            msg_ref[h * (block // per) + d, :, groups * LANES :] = extra.astype(BF16)
    for copy in copies[middle:]:
        copy.wait()
    for h in range(KEY_VALUE_HEADS):
        part = slice(HEAD_DIMENSION * h, HEAD_DIMENSION * (h + 1))
        value = jnp.dot(wides[h], vbuf[:, part], preferred_element_type=F32) * shares[h]
        for d in range(block // per):
            for c in range(groups):
                msg_ref[h * (block // per) + d, :, LANES * c : LANES * (c + 1)] = value[
                    per * d + tall * c : per * d + tall * (c + 1)
                ].astype(BF16)


def project_kernel(arr_ref, own_ref, mine_ref, w_ref, msg_ref, raw_ref, hs, held, placed):
    ranks, tall, across = arr_ref.shape
    groups = across // LANES - 1
    rows, width = mine_ref.shape
    own_heads = tall * groups // rows
    place = lax.axis_index("tok")
    placed[...] = jnp.zeros_like(placed)
    if width % LANES == 0:
        slot = pl.ds(pl.multiple_of(place * width, LANES), width)
        placed[:, slot] = mine_ref[...].astype(F32)
    else:
        for b in range(ranks):

            @pl.when(place == b)
            def _():
                placed[:, b * width : (b + 1) * width] = mine_ref[...].astype(F32)

    lane = lax.broadcasted_iota(jnp.int32, (tall, LANES), 1)
    own_score = jnp.full((tall, LANES), -1e30, F32)
    for c in range(groups):
        own_score = jnp.where(
            lane == 3 * c, own_ref[tall * c : tall * (c + 1), LANES:], own_score
        )
    stats = [arr_ref[b, :, groups * LANES :].astype(F32) for b in range(ranks)]
    top = own_score
    for b in range(ranks):
        top = jnp.maximum(top, stats[b])
    self_weight = jnp.exp(own_score - top)
    below = self_weight
    factors = []
    for b in range(ranks):
        total = pltpu.roll(stats[b], LANES - 1, 1) + pltpu.roll(stats[b], LANES - 2, 1)
        factors.append(total * jnp.exp(stats[b] - top))
        below = below + factors[b]
    for c in range(groups):
        some = slice(tall * c, tall * (c + 1))
        column = slice(3 * c, 3 * c + 1)
        combined = self_weight[:, column] * own_ref[some, :LANES]
        for b in range(ranks):
            combined = combined + factors[b][:, column] * arr_ref[
                b, :, LANES * c : LANES * (c + 1)
            ].astype(F32)
        hs[some, :] = combined / below[:, column]
    heads = jnp.concatenate(
        [hs[rows * j : rows * (j + 1), :] for j in range(own_heads)], axis=1
    ).astype(BF16)
    wide = D // CUTS
    for n in range(CUTS):
        some = slice(wide * n, wide * (n + 1))
        out = jnp.dot(heads, w_ref[:, some], preferred_element_type=F32)
        held[:, some] = out
        sent = (out + placed[:, some]).astype(BF16)
        for b in range(msg_ref.shape[0]):
            msg_ref[b, :, some] = sent
    if width % LANES == 0:
        raw_ref[...] = held[:, slot]
    else:
        for b in range(ranks):

            @pl.when(place == b)
            def _():
                raw_ref[...] = held[:, b * width : (b + 1) * width]


def norm_kernel(arr_ref, raw_ref, gain_ref, att_ref, normed_ref, held):
    rows = raw_ref.shape[0]
    exps = normed_ref.shape[0] // rows
    ranks = arr_ref.shape[0] // exps
    for k in range(exps):
        source = lax.axis_index("exp") ^ k
        hidden = arr_ref[source].astype(F32)
        for b in range(1, ranks):
            hidden = hidden + arr_ref[source + b * exps].astype(F32)
        scale = lax.rsqrt(jnp.sum(hidden * hidden, axis=1, keepdims=True) * (1.0 / D) + 1e-06)
        held[rows * k : rows * (k + 1), :] = hidden * scale * gain_ref[...]
    normed_ref[...] = held[...].astype(BF16)
    width = att_ref.shape[1]
    place = lax.axis_index("tok")
    mine = lax.axis_index("exp")

    def gather(slot):
        total = raw_ref[...]
        for b in range(ranks):
            part = arr_ref[mine + b * exps, :, slot].astype(F32)
            total = total + jnp.where(place == b, 0.0, part)
        att_ref[...] = total

    if width % LANES == 0:
        gather(pl.ds(pl.multiple_of(place * width, LANES), width))
    else:
        for b in range(ranks):
            pl.when(place == b)(functools.partial(gather, slice(b * width, (b + 1) * width)))


def expert_kernel(ids_ref, gates_ref, *refs, packed):
    subs, exps, rows, _ = ids_ref.shape
    sources = refs[:subs]
    wg_ref, wu_ref, wd_ref, out_ref, gains = refs[subs:]
    mine = lax.axis_index("tok") * subs + lax.axis_index("sub")
    for k in range(subs * exps):
        s = lax.axis_index("sub") ^ (k // exps)
        e = lax.axis_index("exp") ^ (k % exps)
        named = jnp.where(ids_ref[s, e] == mine, gates_ref[s, e], 0.0)
        gains[rows * k : rows * (k + 1), :] = jnp.broadcast_to(
            jnp.sum(named, axis=1, keepdims=True), (rows, LANES)
        )
    x = jnp.concatenate([ref[...].astype(F32) for ref in sources], axis=0).astype(BF16)
    gate = jnp.dot(x, wg_ref[0], preferred_element_type=F32)
    up = jnp.dot(x, wu_ref[0], preferred_element_type=F32)
    act = (gate / (1.0 + jnp.exp(-gate)) * up * gains[:, :1]).astype(BF16)
    if not packed:
        out_ref[...] = jnp.dot(act, wd_ref[0], preferred_element_type=F32).astype(BF16)
        return
    half = x.shape[0] // 2
    left = lax.broadcasted_iota(jnp.int32, (half, LANES), 1) < HALF
    wide = D // CUTS
    for n in range(CUTS):
        y = jnp.dot(act, wd_ref[0, :, wide * n : wide * (n + 1)], preferred_element_type=F32)
        for c in range(wide // LANES):
            upper = y[:half, LANES * c : LANES * (c + 1)]
            lower = y[half:, LANES * c : LANES * (c + 1)]
            place = 2 * (wide // LANES * n + c)
            out_ref[place] = jnp.where(left, upper, pltpu.roll(lower, HALF, 1)).astype(BF16)
            out_ref[place + 1] = jnp.where(left, pltpu.roll(upper, HALF, 1), lower).astype(BF16)


def mix_kernel(arr_ref, att_ref, out_ref, final_ref):
    final_ref[...] = att_ref[...]
    subs, exps, rows, _ = out_ref.shape
    ranks = subs * exps
    half = ranks * rows // 2
    totals = []
    for g in range(ranks):
        total = arr_ref[g].astype(F32)
        for b in range(g + ranks, arr_ref.shape[0], ranks):
            total = total + arr_ref[b].astype(F32)
        totals.append(total)
    for j in range(ranks):
        mixed = None
        for g in range(ranks):
            k = j ^ g
            row = ((k % subs) * exps + k // subs) * rows
            lanes = slice(0, HALF) if row < half else slice(HALF, LANES)
            piece = totals[g][row % half : row % half + rows, lanes]
            mixed = piece if mixed is None else mixed + piece
        out_ref[j % subs, j // subs] = mixed


VMEM_SPEC = pl.BlockSpec(memory_space=pltpu.VMEM)
HBM_SPEC = pl.BlockSpec(memory_space=pltpu.HBM)


def call(kernel, shapes, in_specs, scratch, name, cost=0, limit=8 * 1024 * 1024):
    many = isinstance(shapes, (list, tuple))
    return pl.pallas_call(
        kernel,
        out_shape=shapes,
        in_specs=in_specs,
        out_specs=[VMEM_SPEC] * len(shapes) if many else VMEM_SPEC,
        scratch_shapes=scratch,
        name=name,
        cost_estimate=pl.CostEstimate(flops=cost, bytes_accessed=cost // 700, transcendentals=0),
        compiler_params=pltpu.CompilerParams(vmem_limit_bytes=limit),
    )


def body(
    query,
    key_cache_table,
    value_cache_table,
    latest_key,
    latest_value,
    lengths,
    resid,
    norm_gain,
    out_weight,
    expert_ids,
    gate_weights,
    w_gate,
    w_up,
    w_down,
):
    tok_ranks = lax.axis_size("tok")
    exp_ranks = lax.axis_size("exp")
    sub_ranks = lax.axis_size("sub")
    rows = query.shape[2]
    extent = key_cache_table.shape[3]
    feature_cols = resid.shape[3]
    own_heads = QUERY_HEADS // tok_ranks
    per = own_heads * rows
    groups = max(1, per // 8)
    keys = key_cache_table.reshape(rows, extent, KEY_VALUE_HEADS * HEAD_DIMENSION)
    values = value_cache_table.reshape(rows, extent, KEY_VALUE_HEADS * HEAD_DIMENSION)
    q = query.reshape(rows, QUERY_HEADS * HEAD_DIMENSION)
    shared_cols = KEY_VALUE_HEADS * HEAD_DIMENSION
    message, own = call(
        attend_kernel,
        [
            jax.ShapeDtypeStruct((tok_ranks, per // groups, (groups + 1) * LANES), BF16),
            jax.ShapeDtypeStruct((per, 2 * LANES), F32),
        ],
        [HBM_SPEC] * 6,
        [
            pltpu.SMEM(lengths.shape, jnp.int32),
            pltpu.VMEM((rows, QUERY_HEADS * HEAD_DIMENSION), BF16),
            pltpu.VMEM((rows, shared_cols), BF16),
            pltpu.VMEM((rows, shared_cols), BF16),
            pltpu.VMEM((rows * extent, shared_cols), BF16),
            pltpu.VMEM((rows * extent, shared_cols), BF16),
            pltpu.VMEM((QUERY_HEADS * rows, HEAD_DIMENSION), F32),
            pltpu.SemaphoreType.DMA((3,)),
        ],
        "attend",
        cost=20_000_000_000,
    )(
        *(
            pltpu.with_memory_space_constraint(x, pltpu.HBM)
            for x in (
                lengths,
                q,
                latest_key.reshape(rows, shared_cols),
                latest_value.reshape(rows, shared_cols),
                keys,
                values,
            )
        )
    )
    arrived = lax.all_to_all(message, "tok", split_axis=0, concat_axis=0, tiled=True)
    share, raw = call(
        project_kernel,
        [
            jax.ShapeDtypeStruct((tok_ranks * exp_ranks, rows, D), BF16),
            jax.ShapeDtypeStruct((rows, feature_cols), F32),
        ],
        [VMEM_SPEC] * 4,
        [
            pltpu.VMEM((per, LANES), F32),
            pltpu.VMEM((rows, D), F32),
            pltpu.VMEM((rows, D), F32),
        ],
        "project",
        cost=20_000_000_000,
    )(arrived, own, resid.reshape(rows, feature_cols), out_weight)
    shares = lax.all_to_all(share, ("tok", "exp"), split_axis=0, concat_axis=0, tiled=True)
    attended, normed = call(
        norm_kernel,
        [
            jax.ShapeDtypeStruct((rows, feature_cols), F32),
            jax.ShapeDtypeStruct((exp_ranks * rows, D), BF16),
        ],
        [VMEM_SPEC] * 3,
        [pltpu.VMEM((exp_ranks * rows, D), F32)],
        "norm",
    )(shares, raw, norm_gain.reshape(1, D))
    ranks = exp_ranks * sub_ranks
    pieces = [normed] + [
        lax.ppermute(normed, "sub", [(i, i ^ k) for i in range(sub_ranks)])
        for k in range(1, sub_ranks)
    ]
    block_cols = D // (tok_ranks * ranks)
    packed = 2 * block_cols == LANES
    rows_all = ranks * rows
    shape = (tok_ranks * ranks, rows_all // 2, LANES) if packed else (rows_all, D)
    weighted = call(
        functools.partial(expert_kernel, packed=packed),
        jax.ShapeDtypeStruct(shape, BF16),
        [VMEM_SPEC] * (5 + sub_ranks),
        [pltpu.VMEM((rows_all, LANES), F32)],
        "experts",
    )(expert_ids, gate_weights, *pieces, w_gate, w_up, w_down)
    everywhere = ("tok", "exp", "sub")
    if packed:
        received = lax.all_to_all(weighted, everywhere, split_axis=0, concat_axis=0, tiled=True)
        expert_mix, attended = call(
            mix_kernel,
            [
                jax.ShapeDtypeStruct((sub_ranks, exp_ranks, rows, block_cols), F32),
                jax.ShapeDtypeStruct((rows, feature_cols), F32),
            ],
            [VMEM_SPEC] * 2,
            [],
            "mix",
        )(received, attended)
    else:
        blocks = jnp.transpose(weighted.reshape(rows_all, tok_ranks * ranks, block_cols), (1, 0, 2))
        received = lax.all_to_all(blocks, everywhere, split_axis=0, concat_axis=0, tiled=True)
        grouped = jnp.sum(
            received.astype(F32).reshape(tok_ranks, ranks, ranks, rows, block_cols), axis=0
        )
        order = [(k % sub_ranks) * exp_ranks + k // sub_ranks for k in range(ranks)]
        mixed = [sum(grouped[g, order[j ^ g]] for g in range(ranks)) for j in range(ranks)]
        expert_mix = jnp.transpose(
            jnp.stack(mixed).reshape(exp_ranks, sub_ranks, rows, block_cols), (1, 0, 2, 3)
        )
    return (attended.reshape(1, 1, rows, feature_cols), expert_mix)


def solution(mesh):
    placed = (
        P(("groups", "sub"), "exp", None, None),
        P(("groups", "sub"), "exp", None, "tok", None),
        P(("groups", "sub"), "exp", None, "tok", None),
        P(("groups", "sub"), "exp", None, None),
        P(("groups", "sub"), "exp", None, None),
        P(("groups", "sub"), "exp", None),
        P(("groups", "sub"), "exp", None, "tok"),
        P(),
        P("tok", None),
        P("groups", None, None, None),
        P("groups", None, None, None),
        P(("tok", "sub"), None, "exp"),
        P(("tok", "sub"), None, "exp"),
        P(("tok", "sub"), "exp", None),
    )
    return jax.shard_map(
        body,
        mesh=mesh,
        in_specs=placed,
        out_specs=(
            P(("groups", "sub"), "exp", None, "tok"),
            P("groups", None, None, ("tok", "exp", "sub")),
        ),
        check_vma=False,
    )
```

```python
import functools

import jax
import jax.numpy as jnp
from jax import lax
from jax.experimental import pallas as pl
from jax.experimental.pallas import tpu as pltpu
from jax.sharding import PartitionSpec as P

D = 2048
QUERY_HEADS = 32
KEY_VALUE_HEADS = 4
HEAD_DIMENSION = 128
TOPK = 8
GROUP = QUERY_HEADS // KEY_VALUE_HEADS
CUTS = 2
SCALE = HEAD_DIMENSION ** (-0.5)
LANES = 128
HALF = 64
PIECES = 16

F32 = jnp.float32
BF16 = jnp.bfloat16


def attend_kernel(
    len_hbm,
    q_hbm,
    lk_hbm,
    lv_hbm,
    k_hbm,
    v_hbm,
    msg_ref,
    own_ref,
    len_ref,
    q_ref,
    lk_ref,
    lv_ref,
    kbuf,
    vbuf,
    qs,
    sems,
):
    rows = q_ref.shape[0]
    extent = k_hbm.shape[1]
    own_heads = own_ref.shape[0] // rows
    block = GROUP * rows
    cut = extent // PIECES
    copies = [
        pltpu.make_async_copy(source, target, sems.at[0])
        for source, target in (
            (q_hbm, q_ref),
            (len_hbm, len_ref),
            (lk_hbm, lk_ref),
            (lv_hbm, lv_ref),
        )
    ]
    early = len(copies)
    for which, (source, target) in enumerate(((k_hbm, kbuf), (v_hbm, vbuf))):
        for r in range(rows):
            for c in range(PIECES):
                copies.append(
                    pltpu.make_async_copy(
                        source.at[r, pl.ds(cut * c, cut)],
                        target.at[pl.ds(r * extent + cut * c, cut)],
                        sems.at[1 + which],
                    )
                )
    middle = early + rows * PIECES
    for n, copy in enumerate(copies):
        copy.start(priority=1 if n >= middle else 0)
    for copy in copies[:early]:
        copy.wait()
    place = lax.axis_index("tok")
    for h in range(QUERY_HEADS):
        qs[rows * h : rows * (h + 1), :] = q_ref[
            :, HEAD_DIMENSION * h : HEAD_DIMENSION * (h + 1)
        ].astype(F32)
    for j in range(own_heads):
        head = place * own_heads + j
        mine = pl.ds(pl.multiple_of(head * HEAD_DIMENSION, HEAD_DIMENSION), HEAD_DIMENSION)
        shared = pl.ds(
            pl.multiple_of((head // GROUP) * HEAD_DIMENSION, HEAD_DIMENSION), HEAD_DIMENSION
        )
        product = q_ref[:, mine].astype(F32) * lk_ref[:, shared].astype(F32)
        own_ref[rows * j : rows * (j + 1), LANES:] = jnp.broadcast_to(
            jnp.sum(product, axis=1, keepdims=True) * SCALE, (rows, LANES)
        )
        own_ref[rows * j : rows * (j + 1), :LANES] = lv_ref[:, shared].astype(F32)
    row_id = lax.rem(lax.broadcasted_iota(jnp.int32, (block, 1), 0), rows)
    limit = jnp.zeros((block, 1), jnp.int32)
    for r in range(rows):
        limit = jnp.where(row_id == r, len_ref[0, 0, r], limit)
    first = place * extent
    usable = first + lax.broadcasted_iota(jnp.int32, (block, extent), 1) < limit
    queries = [qs[block * h : block * (h + 1), :].astype(BF16) for h in range(KEY_VALUE_HEADS)]
    for copy in copies[early:middle]:
        copy.wait()
    ranks, tall, across = msg_ref.shape
    groups = across // LANES - 1
    per = tall * groups
    lane = lax.broadcasted_iota(jnp.int32, (tall, LANES), 1)
    wides, shares = [], []
    for h in range(KEY_VALUE_HEADS):
        part = slice(HEAD_DIMENSION * h, HEAD_DIMENSION * (h + 1))
        full = lax.dot_general(
            queries[h], kbuf[:, part], (((1,), (1,)), ((), ())), preferred_element_type=F32
        )
        score = full[:, :extent]
        for r in range(1, rows):
            score = jnp.where(row_id == r, full[:, extent * r : extent * (r + 1)], score)
        masked = jnp.where(usable, score * SCALE, -1e30)
        peak = jnp.max(masked, axis=1, keepdims=True).astype(BF16).astype(F32)
        weight = jnp.where(usable, jnp.exp(masked - peak), 0.0).astype(BF16).astype(F32)
        total = jnp.sum(weight, axis=1, keepdims=True)
        wides.append(
            jnp.concatenate(
                [jnp.where(row_id == r, weight, 0.0) for r in range(rows)], axis=1
            ).astype(BF16)
        )
        shares.append(1.0 / jnp.where(total > 0.0, total, 1.0))
        high = total.astype(BF16).astype(F32)
        low = total - high
        for d in range(block // per):
            extra = jnp.zeros((tall, LANES), F32)
            for c in range(groups):
                some = slice(per * d + tall * c, per * d + tall * (c + 1))
                extra = jnp.where(lane == 3 * c, peak[some], extra)
                extra = jnp.where(lane == 3 * c + 1, high[some], extra)
                extra = jnp.where(lane == 3 * c + 2, low[some], extra)
            msg_ref[h * (block // per) + d, :, groups * LANES :] = extra.astype(BF16)
    for copy in copies[middle:]:
        copy.wait()
    for h in range(KEY_VALUE_HEADS):
        part = slice(HEAD_DIMENSION * h, HEAD_DIMENSION * (h + 1))
        value = jnp.dot(wides[h], vbuf[:, part], preferred_element_type=F32) * shares[h]
        for d in range(block // per):
            for c in range(groups):
                msg_ref[h * (block // per) + d, :, LANES * c : LANES * (c + 1)] = value[
                    per * d + tall * c : per * d + tall * (c + 1)
                ].astype(BF16)


def project_kernel(arr_ref, own_ref, mine_ref, w_ref, msg_ref, raw_ref, hs, held, placed):
    ranks, tall, across = arr_ref.shape
    groups = across // LANES - 1
    rows, width = mine_ref.shape
    own_heads = tall * groups // rows
    place = lax.axis_index("tok")
    placed[...] = jnp.zeros_like(placed)
    if width % LANES == 0:
        slot = pl.ds(pl.multiple_of(place * width, LANES), width)
        placed[:, slot] = mine_ref[...].astype(F32)
    else:
        for b in range(ranks):

            @pl.when(place == b)
            def _():
                placed[:, b * width : (b + 1) * width] = mine_ref[...].astype(F32)

    lane = lax.broadcasted_iota(jnp.int32, (tall, LANES), 1)
    own_score = jnp.full((tall, LANES), -1e30, F32)
    for c in range(groups):
        own_score = jnp.where(
            lane == 3 * c, own_ref[tall * c : tall * (c + 1), LANES:], own_score
        )
    stats = [arr_ref[b, :, groups * LANES :].astype(F32) for b in range(ranks)]
    top = own_score
    for b in range(ranks):
        top = jnp.maximum(top, stats[b])
    self_weight = jnp.exp(own_score - top)
    below = self_weight
    factors = []
    for b in range(ranks):
        total = pltpu.roll(stats[b], LANES - 1, 1) + pltpu.roll(stats[b], LANES - 2, 1)
        factors.append(total * jnp.exp(stats[b] - top))
        below = below + factors[b]
    for c in range(groups):
        some = slice(tall * c, tall * (c + 1))
        column = slice(3 * c, 3 * c + 1)
        combined = self_weight[:, column] * own_ref[some, :LANES]
        for b in range(ranks):
            combined = combined + factors[b][:, column] * arr_ref[
                b, :, LANES * c : LANES * (c + 1)
            ].astype(F32)
        hs[some, :] = combined / below[:, column]
    heads = jnp.concatenate(
        [hs[rows * j : rows * (j + 1), :] for j in range(own_heads)], axis=1
    ).astype(BF16)
    wide = D // (2 * CUTS)
    for n in range(2 * CUTS):
        some = slice(wide * n, wide * (n + 1))
        out = jnp.dot(heads, w_ref[:, some], preferred_element_type=F32)
        held[:, some] = out
        sent = (out + placed[:, some]).astype(BF16)
        for b in range(msg_ref.shape[0]):
            msg_ref[b, :, some] = sent
    if width % LANES == 0:
        raw_ref[...] = held[:, slot]
    else:
        for b in range(ranks):

            @pl.when(place == b)
            def _():
                raw_ref[...] = held[:, b * width : (b + 1) * width]


def norm_kernel(arr_ref, raw_ref, gain_ref, att_ref, normed_ref, held):
    rows = raw_ref.shape[0]
    exps = normed_ref.shape[0] // rows
    ranks = arr_ref.shape[0] // exps
    for k in range(exps):
        source = lax.axis_index("exp") ^ k
        hidden = arr_ref[source].astype(F32)
        for b in range(1, ranks):
            hidden = hidden + arr_ref[source + b * exps].astype(F32)
        scale = lax.rsqrt(jnp.sum(hidden * hidden, axis=1, keepdims=True) * (1.0 / D) + 1e-06)
        held[rows * k : rows * (k + 1), :] = hidden * scale * gain_ref[...]
    normed_ref[...] = held[...].astype(BF16)
    width = att_ref.shape[1]
    place = lax.axis_index("tok")
    mine = lax.axis_index("exp")

    def gather(slot):
        total = raw_ref[...]
        for b in range(ranks):
            part = arr_ref[mine + b * exps, :, slot].astype(F32)
            total = total + jnp.where(place == b, 0.0, part)
        att_ref[...] = total

    if width % LANES == 0:
        gather(pl.ds(pl.multiple_of(place * width, LANES), width))
    else:
        for b in range(ranks):
            pl.when(place == b)(functools.partial(gather, slice(b * width, (b + 1) * width)))


def expert_kernel(ids_ref, gates_ref, *refs, packed):
    subs, exps, rows, _ = ids_ref.shape
    sources = refs[:subs]
    wg_ref, wu_ref, wd_ref, out_ref, gains = refs[subs:]
    mine = lax.axis_index("tok") * subs + lax.axis_index("sub")
    for k in range(subs * exps):
        s = lax.axis_index("sub") ^ (k // exps)
        e = lax.axis_index("exp") ^ (k % exps)
        named = jnp.where(ids_ref[s, e] == mine, gates_ref[s, e], 0.0)
        gains[rows * k : rows * (k + 1), :] = jnp.broadcast_to(
            jnp.sum(named, axis=1, keepdims=True), (rows, LANES)
        )
    x = jnp.concatenate([ref[...] for ref in sources], axis=0)
    gate = jnp.dot(x, wg_ref[0], preferred_element_type=F32)
    up = jnp.dot(x, wu_ref[0], preferred_element_type=F32)
    act = (gate / (1.0 + jnp.exp(-gate)) * up * gains[:, :1]).astype(BF16)
    if not packed:
        out_ref[...] = jnp.dot(act, wd_ref[0], preferred_element_type=F32).astype(BF16)
        return
    half = x.shape[0] // 2
    left = lax.broadcasted_iota(jnp.int32, (half, LANES), 1) < HALF
    wide = D // CUTS
    for n in range(CUTS):
        y = jnp.dot(act, wd_ref[0, :, wide * n : wide * (n + 1)], preferred_element_type=F32)
        for c in range(wide // LANES):
            upper = y[:half, LANES * c : LANES * (c + 1)]
            lower = y[half:, LANES * c : LANES * (c + 1)]
            place = 2 * (wide // LANES * n + c)
            out_ref[place] = jnp.where(left, upper, pltpu.roll(lower, HALF, 1)).astype(BF16)
            out_ref[place + 1] = jnp.where(left, pltpu.roll(upper, HALF, 1), lower).astype(BF16)


def mix_kernel(arr_ref, att_ref, out_ref, final_ref):
    final_ref[...] = att_ref[...]
    subs, exps, rows, _ = out_ref.shape
    ranks = subs * exps
    half = ranks * rows // 2
    totals = []
    for g in range(ranks):
        total = arr_ref[g].astype(F32)
        for b in range(g + ranks, arr_ref.shape[0], ranks):
            total = total + arr_ref[b].astype(F32)
        totals.append(total)
    for j in range(ranks):
        mixed = None
        for g in range(ranks):
            k = j ^ g
            row = ((k % subs) * exps + k // subs) * rows
            lanes = slice(0, HALF) if row < half else slice(HALF, LANES)
            piece = totals[g][row % half : row % half + rows, lanes]
            mixed = piece if mixed is None else mixed + piece
        out_ref[j % subs, j // subs] = mixed


VMEM_SPEC = pl.BlockSpec(memory_space=pltpu.VMEM)
HBM_SPEC = pl.BlockSpec(memory_space=pltpu.HBM)


def call(kernel, shapes, in_specs, scratch, name, cost=0, limit=8 * 1024 * 1024):
    many = isinstance(shapes, (list, tuple))
    return pl.pallas_call(
        kernel,
        out_shape=shapes,
        in_specs=in_specs,
        out_specs=[VMEM_SPEC] * len(shapes) if many else VMEM_SPEC,
        scratch_shapes=scratch,
        name=name,
        cost_estimate=pl.CostEstimate(flops=cost, bytes_accessed=cost // 700, transcendentals=0),
        compiler_params=pltpu.CompilerParams(vmem_limit_bytes=limit),
    )


def body(
    query,
    key_cache_table,
    value_cache_table,
    latest_key,
    latest_value,
    lengths,
    resid,
    norm_gain,
    out_weight,
    expert_ids,
    gate_weights,
    w_gate,
    w_up,
    w_down,
):
    tok_ranks = lax.axis_size("tok")
    exp_ranks = lax.axis_size("exp")
    sub_ranks = lax.axis_size("sub")
    rows = query.shape[2]
    extent = key_cache_table.shape[3]
    feature_cols = resid.shape[3]
    own_heads = QUERY_HEADS // tok_ranks
    per = own_heads * rows
    groups = max(1, per // 8)
    keys = key_cache_table.reshape(rows, extent, KEY_VALUE_HEADS * HEAD_DIMENSION)
    values = value_cache_table.reshape(rows, extent, KEY_VALUE_HEADS * HEAD_DIMENSION)
    q = query.reshape(rows, QUERY_HEADS * HEAD_DIMENSION)
    shared_cols = KEY_VALUE_HEADS * HEAD_DIMENSION
    message, own = call(
        attend_kernel,
        [
            jax.ShapeDtypeStruct((tok_ranks, per // groups, (groups + 1) * LANES), BF16),
            jax.ShapeDtypeStruct((per, 2 * LANES), F32),
        ],
        [HBM_SPEC] * 6,
        [
            pltpu.SMEM(lengths.shape, jnp.int32),
            pltpu.VMEM((rows, QUERY_HEADS * HEAD_DIMENSION), BF16),
            pltpu.VMEM((rows, shared_cols), BF16),
            pltpu.VMEM((rows, shared_cols), BF16),
            pltpu.VMEM((rows * extent, shared_cols), BF16),
            pltpu.VMEM((rows * extent, shared_cols), BF16),
            pltpu.VMEM((QUERY_HEADS * rows, HEAD_DIMENSION), F32),
            pltpu.SemaphoreType.DMA((3,)),
        ],
        "attend",
        cost=20_000_000_000,
    )(
        *(
            pltpu.with_memory_space_constraint(x, pltpu.HBM)
            for x in (
                lengths,
                q,
                latest_key.reshape(rows, shared_cols),
                latest_value.reshape(rows, shared_cols),
                keys,
                values,
            )
        )
    )
    arrived = lax.all_to_all(message, "tok", split_axis=0, concat_axis=0, tiled=True)
    share, raw = call(
        project_kernel,
        [
            jax.ShapeDtypeStruct((tok_ranks * exp_ranks, rows, D), BF16),
            jax.ShapeDtypeStruct((rows, feature_cols), F32),
        ],
        [VMEM_SPEC] * 4,
        [
            pltpu.VMEM((per, LANES), F32),
            pltpu.VMEM((rows, D), F32),
            pltpu.VMEM((rows, D), F32),
        ],
        "project",
        cost=20_000_000_000,
    )(arrived, own, resid.reshape(rows, feature_cols), out_weight)
    shares = lax.all_to_all(share, ("tok", "exp"), split_axis=0, concat_axis=0, tiled=True)
    attended, normed = call(
        norm_kernel,
        [
            jax.ShapeDtypeStruct((rows, feature_cols), F32),
            jax.ShapeDtypeStruct((exp_ranks * rows, D), BF16),
        ],
        [VMEM_SPEC] * 3,
        [pltpu.VMEM((exp_ranks * rows, D), F32)],
        "norm",
    )(shares, raw, norm_gain.reshape(1, D))
    ranks = exp_ranks * sub_ranks
    pieces = [normed] + [
        lax.ppermute(normed, "sub", [(i, i ^ k) for i in range(sub_ranks)])
        for k in range(1, sub_ranks)
    ]
    block_cols = D // (tok_ranks * ranks)
    packed = 2 * block_cols == LANES
    rows_all = ranks * rows
    shape = (tok_ranks * ranks, rows_all // 2, LANES) if packed else (rows_all, D)
    weighted = call(
        functools.partial(expert_kernel, packed=packed),
        jax.ShapeDtypeStruct(shape, BF16),
        [VMEM_SPEC] * (5 + sub_ranks),
        [pltpu.VMEM((rows_all, LANES), F32)],
        "experts",
    )(expert_ids, gate_weights, *pieces, w_gate, w_up, w_down)
    everywhere = ("tok", "exp", "sub")
    if packed:
        received = lax.all_to_all(weighted, everywhere, split_axis=0, concat_axis=0, tiled=True)
        expert_mix, attended = call(
            mix_kernel,
            [
                jax.ShapeDtypeStruct((sub_ranks, exp_ranks, rows, block_cols), F32),
                jax.ShapeDtypeStruct((rows, feature_cols), F32),
            ],
            [VMEM_SPEC] * 2,
            [],
            "mix",
        )(received, attended)
    else:
        blocks = jnp.transpose(weighted.reshape(rows_all, tok_ranks * ranks, block_cols), (1, 0, 2))
        received = lax.all_to_all(blocks, everywhere, split_axis=0, concat_axis=0, tiled=True)
        grouped = jnp.sum(
            received.astype(F32).reshape(tok_ranks, ranks, ranks, rows, block_cols), axis=0
        )
        order = [(k % sub_ranks) * exp_ranks + k // sub_ranks for k in range(ranks)]
        mixed = [sum(grouped[g, order[j ^ g]] for g in range(ranks)) for j in range(ranks)]
        expert_mix = jnp.transpose(
            jnp.stack(mixed).reshape(exp_ranks, sub_ranks, rows, block_cols), (1, 0, 2, 3)
        )
    return (attended.reshape(1, 1, rows, feature_cols), expert_mix)


def solution(mesh):
    placed = (
        P(("groups", "sub"), "exp", None, None),
        P(("groups", "sub"), "exp", None, "tok", None),
        P(("groups", "sub"), "exp", None, "tok", None),
        P(("groups", "sub"), "exp", None, None),
        P(("groups", "sub"), "exp", None, None),
        P(("groups", "sub"), "exp", None),
        P(("groups", "sub"), "exp", None, "tok"),
        P(),
        P("tok", None),
        P("groups", None, None, None),
        P("groups", None, None, None),
        P(("tok", "sub"), None, "exp"),
        P(("tok", "sub"), None, "exp"),
        P(("tok", "sub"), "exp", None),
    )
    return jax.shard_map(
        body,
        mesh=mesh,
        in_specs=placed,
        out_specs=(
            P(("groups", "sub"), "exp", None, "tok"),
            P("groups", None, None, ("tok", "exp", "sub")),
        ),
        check_vma=False,
    )
```
